32 devices in a mesh: grp: 2 (over x), row: 16 (over z, y, core).
Axes of the slice: x: 2, y: 2, z: 4, core: 2. Of those that a mesh axis runs over, the one named last changes fastest.
Arguments:
- latent: bfloat16 [4, 16, 48, 16], P('grp', 'row'), parts along dimension 0, may hold values from -70 to 70
- w_in: bfloat16 [27, 16, 512], replicated, may hold values from -0.3125 to 0.3125
- gain_in: float32 [512], replicated, may hold values from 0.25 to 1.75
- w_query: bfloat16 [512, 512], replicated, may hold values from -0.2298097 to 0.2298097
- w_key: bfloat16 [512, 512], replicated, may hold values from -1.45840774 to 1.45840774
- w_value: bfloat16 [512, 512], replicated, may hold values from -0.25 to 0.25
- w_out: bfloat16 [512, 512], replicated, may hold values from -0.25 to 0.25
- gain_up: float32 [512], replicated, may hold values from 0.25 to 1.75
- w_up: bfloat16 [27, 512, 512], P(None, 'row'), may hold values from -0.0546875 to 0.0546875
Outputs:
- decoded: bfloat16 [4, 32, 96, 512], P('grp', 'row'), parts along dimension 0
The draws below stay inside these ranges and needn't reach their ends.
There are 2 independent parts, one for each index of `grp`. The reference program is written for one: setup_inputs(seed, part) draws one part's arguments, and reference() takes and returns one part's arrays. A program takes and returns all parts, laid end to end along the dimension named above; an argument that names none is the same for every part. Nothing has to cross between parts.
All inputs are finite; a program needn't handle non-finite values.
Results may differ from the reference program's by a relative error of at most 0.015.
Values may be sent and summed in bfloat16 or wider, within the bound.
No kernel may reach another device: no remote copies, remote signals or barrier semaphores. Data moves between devices by JAX's collectives and lax.ppermute only.
A program may use at most 128 MiB of HBM per device.

```python
import math
import jax
import jax.numpy as jnp
from jax import lax

D = 512
ZC = 16
GROUPS = 32
FRAMES = 2
COLS = 48
ROWS = 16


def draw_latent(key, part):
    key_base = jax.random.fold_in(key, 21)
    key_cols = jax.random.fold_in(key, 22)
    key_order = jax.random.fold_in(key, 23)
    col_scale = jnp.exp(jax.random.uniform(key_cols, (COLS,), jnp.float32, 0.0, math.log(4.0)))
    shape = (FRAMES, ROWS, COLS, ZC)
    shuffled = jax.random.permutation(key_order, ROWS).astype(jnp.float32) / max(ROWS - 1, 1)
    rising = jnp.exp(math.log(3.0) * shuffled)
    base = jax.random.truncated_normal(key_base, -4.0, 4.0, shape, jnp.float32)
    values = base * rising[None, :, None, None] * col_scale[None, None, :, None]
    return values.astype(jnp.bfloat16)


def shared_query(key):
    raw = jax.random.truncated_normal(jax.random.fold_in(key, 11), -4.0, 4.0, (D, D), jnp.float32)
    return raw * (1.3 / math.sqrt(D))


def draw_w_query(key, part):
    return shared_query(key).astype(jnp.bfloat16)


def draw_w_key(key, part):
    raw = jax.random.truncated_normal(jax.random.fold_in(key, 12), -4.0, 4.0, (D, D), jnp.float32)
    values = raw * (1.3 / math.sqrt(D))
    return values.astype(jnp.bfloat16)


def block_scale(key, extent, shards, smallest, top_value):
    def one(dim, blocks):
        steps = jax.random.uniform(jax.random.fold_in(jax.random.fold_in(key, 6), dim), (blocks,), jnp.float32, smallest / len(shards), top_value / len(shards))
        return jnp.repeat(jnp.exp(steps), extent[dim] // blocks).reshape((-1,) + (1,) * (len(extent) - dim - 1))

    factor_of = one(*shards[0])
    for cut in shards[1:]:
        factor_of = factor_of * one(*cut)
    return factor_of


def scatter_about(key, dims, deviation, most, cuts=(), held_as=jnp.bfloat16):
    level = block_scale(key, dims, cuts, -0.22, 0.18) if cuts else 1.0
    array = jax.random.normal(key, dims, jnp.float32) * deviation * level
    return jnp.minimum(jnp.maximum(array, -most), most).astype(held_as)


def setup_inputs(seed: int = 0, part: int = 0) -> dict:
    arg_keys = jax.random.split(jax.random.key(seed), 10)
    part_splits = jax.random.split(jax.random.fold_in(arg_keys[9], part), 10)
    latent = draw_latent(jax.random.fold_in(jax.random.fold_in(arg_keys[9], part), 71), part)
    w_in = scatter_about(arg_keys[1], (27, ZC, D), (27 * ZC) ** -0.5, 0.3125)
    gain_in = jnp.clip(1.0 + 0.15 * jax.random.normal(arg_keys[2], (D,), jnp.float32), 0.25, 1.75)
    w_query = draw_w_query(jax.random.fold_in(arg_keys[9], 71), part)
    w_key = draw_w_key(jax.random.fold_in(arg_keys[9], 71), part)
    w_value = scatter_about(arg_keys[5], (D, D), D ** -0.5, 0.25)
    w_out = scatter_about(arg_keys[6], (D, D), D ** -0.5, 0.25)
    gain_up = jnp.clip(1.0 + 0.15 * jax.random.normal(arg_keys[7], (D,), jnp.float32), 0.25, 1.75)
    w_up = scatter_about(arg_keys[8], (27, D, D), (27 * D) ** -0.5, 0.0546875, ((1, 16),))
    return {"latent": latent, "w_in": w_in, "gain_in": gain_in, "w_query": w_query, "w_key": w_key, "w_value": w_value, "w_out": w_out, "gain_up": gain_up, "w_up": w_up}


norm_eps = 1e-06

def causal_conv(volume, weight):
    frame_count, row_count, col_count, _ = volume.shape
    spaced = jnp.pad(volume, ((0, 0), (1, 1), (1, 1), (0, 0)))
    first_frame = spaced[:1]
    padded = jnp.concatenate([first_frame, first_frame, spaced], axis=0)
    running = jnp.zeros((frame_count * row_count * col_count, weight.shape[2]), jnp.float32)
    for frame_tap in range(3):
        for row_tap in range(3):
            for col_tap in range(3):
                tap_index = (frame_tap * 3 + row_tap) * 3 + col_tap
                window = padded[frame_tap:frame_tap + frame_count, row_tap:row_tap + row_count, col_tap:col_tap + col_count]
                window = window.reshape(frame_count * row_count * col_count, -1)
                running = running + jnp.dot(window, weight[tap_index], preferred_element_type=jnp.float32)
    return running.reshape(frame_count, row_count, col_count, -1)

def group_norm(volume, gain):
    as_float = volume.astype(jnp.float32)
    grouped = as_float.reshape(volume.shape[:3] + (GROUPS, -1))
    group_avg = lax.optimization_barrier(jnp.mean(grouped, axis=(0, 1, 2, 4), keepdims=True))
    centred = grouped - group_avg
    variance = lax.optimization_barrier(jnp.mean(centred * centred, axis=(0, 1, 2, 4), keepdims=True))
    normal_part = (centred / jnp.sqrt(variance + norm_eps)).reshape(volume.shape)
    return normal_part * gain

def reference(latent, w_in, gain_in, w_query, w_key, w_value, w_out, gain_up, w_up):
    first_out = causal_conv(latent, w_in).astype(jnp.bfloat16)
    normed = group_norm(first_out, gain_in).astype(jnp.bfloat16)
    flat_rows = normed.reshape(-1, D)

    def project(weight):
        result = jnp.dot(flat_rows, weight, preferred_element_type=jnp.float32)
        return result.astype(jnp.bfloat16).reshape(FRAMES, ROWS * COLS, D)
    queries = project(w_query)
    key_table = project(w_key)
    value_table = project(w_value)
    score_scale = 1.0 / math.sqrt(D)
    outputs = []
    for frame_number in range(FRAMES):
        scores = jnp.dot(queries[frame_number], key_table[frame_number].T, preferred_element_type=jnp.float32) * score_scale
        row_peak = lax.optimization_barrier(jnp.max(scores, axis=-1, keepdims=True))
        expo = jnp.exp(scores - row_peak)
        mixed = jnp.dot(expo.astype(jnp.bfloat16), value_table[frame_number], preferred_element_type=jnp.float32)
        mixed = mixed / lax.optimization_barrier(jnp.sum(expo, axis=-1, keepdims=True))
        outputs.append(mixed.astype(jnp.bfloat16))
    attended = jnp.stack(outputs).reshape(-1, D)
    added = first_out.astype(jnp.float32).reshape(-1, D) + jnp.dot(attended, w_out, preferred_element_type=jnp.float32)
    added = added.astype(jnp.bfloat16).reshape(FRAMES, ROWS, COLS, D)
    upsampled = jnp.repeat(jnp.repeat(added, 2, axis=1), 2, axis=2)
    convolved = causal_conv(upsampled, w_up).astype(jnp.bfloat16)
    return jax.nn.silu(group_norm(convolved, gain_up)).astype(jnp.bfloat16)
```

```python
import functools
import math

import jax
import jax.numpy as jnp
import numpy as np
from jax import lax
from jax.experimental import pallas as pl
from jax.experimental.pallas import tpu as pltpu
from jax.sharding import PartitionSpec as P

GROUPS = 32


norm_eps = 1e-06


def extended(cells, sides, width):
    for axis, dim in sides:
        count = lax.axis_size(axis)
        ends = count - 1
        head = lax.slice_in_dim(cells, 0, width, axis=dim)
        tail = lax.slice_in_dim(cells, cells.shape[dim] - width, cells.shape[dim], axis=dim)
        cells = jnp.concatenate(
            [
                lax.ppermute(tail, axis, [(i, (i + 1) % count) for i in range(ends)]),
                cells,
                lax.ppermute(head, axis, [((i + 1) % count, i) for i in range(ends)]),
            ],
            axis=dim,
        )
    return cells


def pad_field(rimmed):
    spaced = jnp.pad(rimmed, ((0, 0), (0, 0), (1, 1), (0, 0)))
    first_frame = spaced[:1]
    return jnp.concatenate([first_frame, first_frame, spaced], axis=0)


def tap_windows(padded, frame_count, row_count, col_count):
    windows = []
    for frame_tap in range(3):
        for row_tap in range(3):
            for col_tap in range(3):
                windows.append(
                    padded[
                        frame_tap : frame_tap + frame_count,
                        row_tap : row_tap + row_count,
                        col_tap : col_tap + col_count,
                    ]
                )
    stacked = jnp.stack(windows, axis=3)
    return stacked.reshape(frame_count * row_count * col_count, -1)


def tap_products(padded, weight, frame_count, row_count, col_count):
    running = jnp.zeros((frame_count * row_count * col_count, weight.shape[2]), jnp.float32)
    for frame_tap in range(3):
        for row_tap in range(3):
            for col_tap in range(3):
                tap_index = (frame_tap * 3 + row_tap) * 3 + col_tap
                window = padded[
                    frame_tap : frame_tap + frame_count,
                    row_tap : row_tap + row_count,
                    col_tap : col_tap + col_count,
                ]
                window = window.reshape(frame_count * row_count * col_count, -1)
                running = running + jnp.dot(
                    window, weight[tap_index], preferred_element_type=jnp.float32
                )
    return running


def group_norm(volume, gain):
    grouped = volume.astype(jnp.float32).reshape(volume.shape[:3] + (GROUPS, -1))
    entry_count = (
        volume.shape[0]
        * volume.shape[1]
        * lax.axis_size("row")
        * volume.shape[2]
        * grouped.shape[4]
    )
    group_total = lax.psum(jnp.sum(grouped, axis=(0, 1, 2, 4)), "row")
    group_avg = group_total / entry_count
    centred = grouped - group_avg[:, None]
    variance = lax.psum(jnp.sum(centred * centred, axis=(0, 1, 2, 4)), "row") / entry_count
    normal_part = centred * lax.rsqrt(variance + norm_eps)[:, None]
    return normal_part.reshape(volume.shape) * gain


def per_device(latent, w_in, gain_in, w_query, w_key, w_value, w_out, gain_up, w_up):
    frame_count, row_count, col_count, _ = latent.shape
    chan_width = w_query.shape[0]
    rimmed = extended(latent, (("row", 1),), 1)
    first_out = jnp.dot(
        tap_windows(pad_field(rimmed), frame_count, row_count, col_count),
        w_in.reshape(-1, chan_width),
        preferred_element_type=jnp.float32,
    )
    first_out = first_out.astype(jnp.bfloat16).reshape(
        frame_count, row_count, col_count, chan_width
    )
    normed = group_norm(first_out, gain_in).astype(jnp.bfloat16)
    flat_rows = normed.reshape(-1, chan_width)
    queries = jnp.dot(flat_rows, w_query, preferred_element_type=jnp.float32).astype(jnp.bfloat16)
    queries = queries.reshape(frame_count, row_count * col_count, chan_width)
    score_scale = 1.0 / math.sqrt(chan_width)
    key_table = jnp.dot(flat_rows, w_key, preferred_element_type=jnp.float32).astype(jnp.bfloat16)
    value_table = jnp.dot(flat_rows, w_value, preferred_element_type=jnp.float32).astype(
        jnp.bfloat16
    )
    key_table = key_table.reshape(frame_count, row_count, col_count, chan_width)
    value_table = value_table.reshape(frame_count, row_count, col_count, chan_width)
    row_peak = jnp.full((frame_count, row_count * col_count), -jnp.inf, jnp.float32)
    denom = jnp.zeros((frame_count, row_count * col_count), jnp.float32)
    weighted = jnp.zeros((frame_count, row_count * col_count, chan_width), jnp.float32)
    scores = (
        jnp.einsum(
            "fqd,fkd->fqk",
            queries,
            lax.all_gather(key_table, "row", axis=1, tiled=True).reshape(
                frame_count, -1, chan_width
            ),
            preferred_element_type=jnp.float32,
        )
        * score_scale
    )
    new_peak = jnp.max(scores, axis=-1)
    correction = jnp.exp(row_peak - new_peak)
    expo = jnp.exp(scores - new_peak[..., None])
    denom = denom * correction + jnp.sum(expo, axis=-1)
    weighted = weighted * correction[..., None] + jnp.einsum(
        "fqk,fkd->fqd",
        expo.astype(jnp.bfloat16),
        lax.all_gather(value_table, "row", axis=1, tiled=True).reshape(frame_count, -1, chan_width),
        preferred_element_type=jnp.float32,
    )
    row_peak, denom, weighted = (new_peak, denom, weighted)
    attended = (weighted / denom[..., None]).astype(jnp.bfloat16).reshape(-1, chan_width)
    added = first_out.astype(jnp.float32).reshape(-1, chan_width) + jnp.dot(
        attended, w_out, preferred_element_type=jnp.float32
    )
    added = added.astype(jnp.bfloat16).reshape(frame_count, row_count, col_count, chan_width)
    full_up = lax.all_gather(w_up, "row", axis=1, tiled=True)
    upsampled = jnp.repeat(jnp.repeat(added, 2, axis=1), 2, axis=2)
    up_rimmed = extended(upsampled, (("row", 1),), 1)
    padded_up = pad_field(up_rimmed)
    running = tap_products(padded_up, full_up, frame_count, 2 * row_count, 2 * col_count)
    convolved = running.astype(jnp.bfloat16).reshape(
        frame_count, 2 * row_count, 2 * col_count, chan_width
    )
    return jax.nn.silu(group_norm(convolved, gain_up)).astype(jnp.bfloat16)


LANES = 128
VMEM_LIMIT = 56 * 1024 * 1024


def lane_iota(width):
    return lax.broadcasted_iota(jnp.int32, (1, width), 1)


def swap_blocks(arrays, width):
    arrays = list(arrays)
    block = lane_iota(LANES) // width
    step = 1
    while step < len(arrays):
        low = (block & step) == 0
        for t in range(len(arrays)):
            if t & step == 0:
                a, b = arrays[t], arrays[t | step]
                arrays[t] = jnp.where(low, a, pltpu.roll(b, step * width, 1))
                arrays[t | step] = jnp.where(low, pltpu.roll(a, LANES - step * width, 1), b)
        step *= 2
    return arrays


def group_sum(row, group):
    width = row.shape[1]
    lane = lane_iota(width)
    step = 1
    while step < group:
        low = (lane & step) == 0
        row = row + jnp.where(
            low, pltpu.roll(row, width - step, 1), pltpu.roll(row, step, 1)
        )
        step *= 2
    return row


def fold_rows(block):
    return jnp.sum(block.reshape(-1, 8, block.shape[1]), axis=0)


def all_rows(part):
    return jnp.broadcast_to(jnp.sum(part, axis=0, keepdims=True), part.shape)


def pack_kernel(w_ref, out_ref):
    taps, _, chan_width = w_ref.shape
    share = chan_width // out_ref.shape[0]
    blocks = LANES // share
    for g in range(out_ref.shape[2] // LANES):
        for col in range(chan_width // LANES):
            pieces = []
            for k in range(blocks):
                tap = g * blocks + k
                if tap < taps:
                    pieces.append(
                        w_ref[tap, :, col * LANES : (col + 1) * LANES].astype(jnp.float32)
                    )
                else:
                    pieces.append(jnp.zeros_like(pieces[0]))
            for d, piece in enumerate(swap_blocks(pieces, share)):
                out_ref[col * blocks + d, :, g * LANES : (g + 1) * LANES] = piece.astype(
                    out_ref.dtype
                )


def mid_kernel(
    dims, z_ref, spread_ref, w_in_ref, gain_ref, wq_ref, wk_ref, wv_ref, wo_ref, out_ref,
    z32, x32, wide, edge, h_ref, q_ref, k_ref, v_ref,
):
    frames, rows, cols, zc, chan, chunk = dims
    per_frame = rows * cols
    total = frames * per_frame
    packed = LANES // zc
    units = cols // packed
    unit_rows = z_ref.shape[0] // rows
    taps_lanes = 9 * zc
    z32[...] = z_ref[...].astype(jnp.float32)
    keep = (lax.broadcasted_iota(jnp.int32, (packed, LANES), 1) // zc) == (
        lax.broadcasted_iota(jnp.int32, (packed, LANES), 0)
    )

    def unpack(i, _):
        for f in range(frames):
            for m in range(units):
                row = z32[pl.ds(i * unit_rows + f * units + m, 1), :]
                at = pl.multiple_of(f * per_frame + i * cols + m * packed, packed)
                x32[pl.ds(at, packed), :] = jnp.where(
                    keep, jnp.broadcast_to(row, (packed, LANES)), 0.0
                )
        return 0

    lax.fori_loop(0, rows, unpack, 0)

    lane = lane_iota(wide.shape[1])
    col_tap = (lane // zc) % 3
    row_tap = (lane // zc) // 3
    col_index = lax.broadcasted_iota(jnp.int32, (cols, 1), 0)
    blank = jnp.zeros((cols, edge.shape[2]), jnp.float32)
    for f in range(frames):
        edge[f, 0:cols, :] = blank
        edge[f, (rows + 1) * cols : (rows + 2) * cols, :] = blank

        def columns(i, _):
            at = pl.multiple_of(f * per_frame + i * cols, 8)
            v = jnp.dot(
                x32[pl.ds(at, cols), :].astype(jnp.bfloat16),
                spread_ref[...],
                preferred_element_type=jnp.float32,
            )
            before = jnp.where(col_index == 0, 0.0, pltpu.roll(v, 1, 0))
            after = jnp.where(col_index == cols - 1, 0.0, pltpu.roll(v, cols - 1, 0))
            v = jnp.where(col_tap == 0, before, jnp.where(col_tap == 2, after, v))
            edge[f, pl.ds(pl.multiple_of((i + 1) * cols, 8), cols), :] = v
            return 0

        lax.fori_loop(0, rows, columns, 0, unroll=2)

        def lines(i, _):
            at = pl.multiple_of(i * cols, 8)
            above = edge[f, pl.ds(at, cols), :]
            here = edge[f, pl.ds(pl.multiple_of(at + cols, 8), cols), :]
            below = edge[f, pl.ds(pl.multiple_of(at + 2 * cols, 8), cols), :]
            v = jnp.where(row_tap == 0, above, jnp.where(row_tap == 2, below, here))
            wide[pl.ds(pl.multiple_of(f * per_frame + at, 16), cols), :] = v.astype(wide.dtype)
            return 0

        lax.fori_loop(0, rows, lines, 0, unroll=2)

    depth = wide.shape[1]

    def first(c, part):
        for f in range(frames):
            acc = None
            for dt in range(3):
                source = max(f + dt - 2, 0)
                at = pl.multiple_of(source * per_frame + c * chunk, 16)
                term = jnp.dot(
                    wide[pl.ds(at, chunk), :],
                    w_in_ref[dt * depth : (dt + 1) * depth, :],
                    preferred_element_type=jnp.float32,
                )
                acc = term if acc is None else acc + term
            acc = acc.astype(jnp.bfloat16)
            h_ref[pl.ds(pl.multiple_of(f * per_frame + c * chunk, 16), chunk), :] = acc
            part = part + fold_rows(acc.astype(jnp.float32))
        return part

    zero = jnp.zeros((8, chan), jnp.float32)
    part = lax.fori_loop(0, per_frame // chunk, first, zero)
    group = chan // GROUPS
    count = total * group
    mean = group_sum(all_rows(part), group) / count
    mean_row = mean[0:1]

    def spreadness(c, part):
        v = h_ref[pl.ds(pl.multiple_of(c * chunk, 16), chunk), :].astype(jnp.float32) - mean_row
        return part + fold_rows(v * v)

    part = lax.fori_loop(0, total // chunk, spreadness, zero)
    variance = group_sum(all_rows(part), group) / count
    scale_row = lax.rsqrt(variance + norm_eps)[0:1]
    gain_row = gain_ref[...]

    def project(c, _):
        at = pl.ds(pl.multiple_of(c * chunk, 16), chunk)
        v = h_ref[at, :].astype(jnp.float32) - mean_row
        normed = (v * scale_row * gain_row).astype(jnp.bfloat16)
        for w, o in ((wq_ref, q_ref), (wk_ref, k_ref), (wv_ref, v_ref)):
            o[at, :] = jnp.dot(normed, w[...], preferred_element_type=jnp.float32).astype(
                jnp.bfloat16
            )
        return 0

    lax.fori_loop(0, total // chunk, project, 0)
    score_scale = 1.0 / math.sqrt(chan)

    def attend(c, _):
        for f in range(frames):
            at = pl.ds(pl.multiple_of(f * per_frame + c * chunk, 16), chunk)
            span = slice(f * per_frame, (f + 1) * per_frame)
            scores = lax.dot_general(
                q_ref[at, :],
                k_ref[span, :],
                (((1,), (1,)), ((), ())),
                preferred_element_type=jnp.float32,
            )
            peak = jnp.max(scores, axis=-1, keepdims=True)
            expo = jnp.exp((scores - peak) * score_scale)
            denom = jnp.sum(expo, axis=-1, keepdims=True)
            mixed = jnp.dot(
                expo.astype(jnp.bfloat16), v_ref[span, :], preferred_element_type=jnp.float32
            )
            mixed = (mixed * (1.0 / denom)).astype(jnp.bfloat16)
            shifted = jnp.dot(mixed, wo_ref[...], preferred_element_type=jnp.float32)
            out_ref[at, :] = (h_ref[at, :].astype(jnp.float32) + shifted).astype(jnp.bfloat16)
        return 0

    lax.fori_loop(0, per_frame // chunk, attend, 0)


def up_kernel(
    dims, w_ref, x_ref, s_old_ref, s_new_ref, gain_ref, out_ref,
    fold_all, fold_old, fold_new, t_ref, m0_ref, m2_ref,
):
    frames, rows, cols, chan, share, old_end, new_start, chunk = dims
    per_frame = rows * cols
    width = 4 * share
    for c in range(chan // chunk):
        at = slice(c * chunk, (c + 1) * chunk)
        old = jnp.dot(w_ref[at, :old_end], s_old_ref[...], preferred_element_type=jnp.float32)
        new = jnp.dot(w_ref[at, new_start:], s_new_ref[...], preferred_element_type=jnp.float32)
        fold_old[at, :] = old.astype(jnp.bfloat16)
        fold_new[at, :] = new.astype(jnp.bfloat16)
        fold_all[at, :] = (old + new).astype(jnp.bfloat16)

    def products(c, _):
        at0 = pl.ds(pl.multiple_of(c * chunk, 16), chunk)
        at1 = pl.ds(pl.multiple_of(per_frame + c * chunk, 16), chunk)
        t_ref[at0, :] = jnp.dot(x_ref[at0, :], fold_all[...], preferred_element_type=jnp.float32)
        t_ref[at1, :] = jnp.dot(
            x_ref[at0, :], fold_old[...], preferred_element_type=jnp.float32
        ) + jnp.dot(x_ref[at1, :], fold_new[...], preferred_element_type=jnp.float32)
        return 0

    lax.fori_loop(0, per_frame // chunk, products, 0)
    lane = lane_iota(width)
    right = (lane // share) % 2 == 1
    lower = (lane // share) // 2 == 1
    col_index = lax.broadcasted_iota(jnp.int32, (cols, 1), 0)

    def beside(v):
        before = jnp.where(col_index == 0, 0.0, pltpu.roll(v, 1, 0))
        after = jnp.where(col_index == cols - 1, 0.0, pltpu.roll(v, cols - 1, 0))
        return jnp.where(right, after, before)

    blank = jnp.zeros((cols, width), jnp.float32)
    part = jnp.zeros((8, width), jnp.float32)
    for f in range(frames):
        m2_ref[f, 0:cols, :] = blank
        m2_ref[f, (rows + 1) * cols : (rows + 2) * cols, :] = blank

        def columns(i, _):
            at = pl.ds(pl.multiple_of(f * per_frame + i * cols, 8), cols)
            m0_ref[at, :] = t_ref[at, 0:width] + beside(t_ref[at, width : 2 * width])
            m2_ref[f, pl.ds(pl.multiple_of((i + 1) * cols, 8), cols), :] = t_ref[
                at, 2 * width : 3 * width
            ] + beside(t_ref[at, 3 * width : 4 * width])
            return 0

        lax.fori_loop(0, rows, columns, 0, unroll=2)

        def lines(i, part):
            at = pl.ds(pl.multiple_of(f * per_frame + i * cols, 8), cols)
            above = m2_ref[f, pl.ds(pl.multiple_of(i * cols, 8), cols), :]
            below = m2_ref[f, pl.ds(pl.multiple_of((i + 2) * cols, 8), cols), :]
            v = m0_ref[at, :] + jnp.where(lower, below, above)
            v = v.astype(jnp.bfloat16).astype(jnp.float32)
            m0_ref[at, :] = v
            return part + fold_rows(v)

        part = lax.fori_loop(0, rows, lines, part, unroll=2)

    group = chan // GROUPS
    count = frames * rows * cols * 4 * group

    def grouped(part):
        part = all_rows(part)
        part = part + pltpu.roll(part, 2 * share, 1)
        part = part + pltpu.roll(part, share, 1)
        return group_sum(part, group)

    mean_row = (grouped(part) / count)[0:1]

    def spreadness(i, part):
        v = m0_ref[pl.ds(pl.multiple_of(i * cols, 8), cols), :] - mean_row
        return part + fold_rows(v * v)

    part = lax.fori_loop(
        0, frames * rows, spreadness, jnp.zeros((8, width), jnp.float32), unroll=2
    )
    variance = grouped(part) / count
    scale_row = (lax.rsqrt(variance + norm_eps) * gain_ref[...])[0:1]

    devices = out_ref.shape[0]
    own = rows // devices

    def finish(d, _):
        for f in range(frames):
            for r in range(own):
                at = pl.ds(pl.multiple_of(f * per_frame + (d * own + r) * cols, 8), cols)
                v = (m0_ref[at, :] - mean_row) * scale_row
                v = v / (1.0 + jnp.exp(-v))
                out_ref[d, (f * own + r) * cols : (f * own + r + 1) * cols, :] = v.astype(
                    out_ref.dtype
                )
        return 0

    lax.fori_loop(0, devices, finish, 0, unroll=2)


def place_kernel(share, x_ref, out_ref, line):
    devices = x_ref.shape[0]
    frames, lines, wide_cols, _ = out_ref.shape
    cols = wide_cols // 2
    own = lines // 2
    blocks = LANES // share
    for a in range(devices // blocks):
        for f in range(frames):
            for r in range(own):
                at = slice((f * own + r) * cols, (f * own + r + 1) * cols)
                pieces = swap_blocks(
                    [x_ref[a * blocks + s, at, :].astype(jnp.float32) for s in range(blocks)],
                    share,
                )
                for p in range(2):
                    slot = ((a * frames + f) * own + r) * 2 + p
                    for q in range(2):
                        line[slot, pl.ds(q, cols, stride=2), :] = pieces[2 * p + q]
                    out_ref[f, 2 * r + p, :, a * LANES : (a + 1) * LANES] = line[slot].astype(
                        out_ref.dtype
                    )


def fold_matrices(share, pad_taps):
    full = np.zeros((pad_taps * share, 16 * share), np.float32)
    for tap in range(27):
        di, dj = (tap % 9) // 3, tap % 3
        for p in range(2):
            for q in range(2):
                a, b = (p + di - 1) // 2, (q + dj - 1) // 2
                shift = 2 * (a != 0) + (b != 0)
                for c in range(share):
                    full[tap * share + c, shift * 4 * share + (2 * p + q) * share + c] = 1.0
    old_end = -(-18 * share // LANES) * LANES
    new_start = 18 * share // LANES * LANES
    old = full[:old_end].copy()
    old[18 * share :] = 0.0
    new = full[new_start:].copy()
    new[: 18 * share - new_start] = 0.0
    return jnp.asarray(old, jnp.bfloat16), jnp.asarray(new, jnp.bfloat16), old_end, new_start


def fits(mesh, shapes):
    latent, w_query = shapes
    count = mesh.shape["row"]
    frames, own, cols, zc = latent
    chan = w_query[0]
    rows = own * count
    return (
        frames == 2
        and own == 1
        and count & (count - 1) == 0
        and chan == count * 32
        and LANES % zc == 0
        and LANES // zc == 8
        and cols % 16 == 0
        and (rows * cols) % 256 == 0
        and rows * cols <= 1024
    )


def call(kernel, out_shape, scratch, flops, moved, count):
    return pl.pallas_call(
        kernel,
        out_shape=out_shape,
        in_specs=[pl.BlockSpec(memory_space=pltpu.VMEM)] * count,
        out_specs=pl.BlockSpec(memory_space=pltpu.VMEM),
        scratch_shapes=scratch,
        compiler_params=pltpu.CompilerParams(vmem_limit_bytes=VMEM_LIMIT),
        cost_estimate=pl.CostEstimate(flops=flops, bytes_accessed=moved, transcendentals=0),
    )


def everyone(cells, held):
    count = lax.axis_size("row")
    me = lax.axis_index("row")
    cells = cells[None]
    bit = count // 2
    while bit:
        if bit == 1:
            cells, held = lax.optimization_barrier((cells, held))
        other = lax.ppermute(cells, "row", [(k, k ^ bit) for k in range(count)])
        mine_first = (me // bit) % 2 == 0
        cells = jnp.where(
            mine_first, jnp.stack([cells, other], 1), jnp.stack([other, cells], 1)
        ).reshape((-1,) + cells.shape[1:])
        bit //= 2
    return cells, held


def whole_video(latent, w_in, gain_in, w_query, w_key, w_value, w_out, gain_up, w_up):
    frames, own, cols, zc = latent.shape
    chan = w_query.shape[0]
    count = lax.axis_size("row")
    rows = own * count
    positions = frames * rows * cols
    share = chan // count
    me = lax.axis_index("row")
    blocks = LANES // share
    pad_taps = -(-27 // blocks) * blocks
    f32, bf16 = jnp.float32, jnp.bfloat16
    shape = jax.ShapeDtypeStruct
    chunk = 256

    flat = latent.reshape(-1, LANES)
    unit_rows = -(-flat.shape[0] // 16) * 16
    flat = jnp.pad(flat, ((0, unit_rows - flat.shape[0]), (0, 0)))
    packed = call(
        pack_kernel, shape((count, w_up.shape[1], pad_taps * share), bf16), [], 10**6, 2 * 10**6, 1
    )(w_up)
    gathered, packed = everyone(flat, packed)
    gathered = gathered.reshape(count * unit_rows, LANES)
    weights = lax.all_to_all(packed, "row", 0, 0, tiled=True).reshape(chan, pad_taps * share)

    depth = -(-9 * zc // LANES) * LANES
    spread = np.zeros((LANES, depth), np.float32)
    for k in range(LANES):
        for t in range(9):
            spread[k, t * zc + k % zc] = 1.0
    w_first = jnp.pad(w_in.reshape(3, 9 * zc, chan), ((0, 0), (0, depth - 9 * zc), (0, 0)))
    dims = (frames, rows, cols, zc, chan, chunk)
    added = call(
        functools.partial(mid_kernel, dims),
        shape((positions, chan), bf16),
        [
            pltpu.VMEM((count * unit_rows, LANES), f32),
            pltpu.VMEM((positions, LANES), f32),
            pltpu.VMEM((positions, depth), bf16),
            pltpu.VMEM((frames, (rows + 2) * cols, depth), f32),
        ]
        + [pltpu.VMEM((positions, chan), bf16)] * 4,
        7 * 10**9,
        6 * 10**6,
        8,
    )(
        gathered,
        jnp.asarray(spread, bf16),
        w_first.reshape(3 * depth, chan),
        gain_in.reshape(1, chan),
        w_query,
        w_key,
        w_value,
        w_out,
    )

    s_old, s_new, old_end, new_start = fold_matrices(share, pad_taps)
    gain = jnp.tile(lax.dynamic_slice(gain_up, (me * share,), (share,)), 4).reshape(1, 4 * share)
    dims = (frames, rows, cols, chan, share, old_end, new_start, chunk)
    width = 4 * share
    decoded = call(
        functools.partial(up_kernel, dims),
        shape((count, frames * own * cols, width), bf16),
        [pltpu.VMEM((chan, 4 * width), bf16)] * 3
        + [
            pltpu.VMEM((positions, 4 * width), f32),
            pltpu.VMEM((positions, width), f32),
            pltpu.VMEM((frames, (rows + 2) * cols, width), f32),
        ],
        3 * 10**9,
        5 * 10**6,
        5,
    )(weights, added, s_old, s_new, gain)
    swapped = lax.all_to_all(decoded, "row", 0, 0, tiled=True)
    slots = (count // blocks) * frames * own * 2
    return call(
        functools.partial(place_kernel, share),
        shape((frames, 2 * own, 2 * cols, chan), bf16),
        [pltpu.VMEM((slots, 2 * cols, LANES), f32)],
        10**6,
        10**6,
        1,
    )(swapped)


def solution(mesh):
    def body(*args):
        whole = fits(mesh, (args[0].shape, args[3].shape))
        return (whole_video if whole else per_device)(*args)

    in_specs = (
        P("grp", "row", None, None),
        P(),
        P(),
        P(),
        P(),
        P(),
        P(),
        P(),
        P(None, "row", None),
    )
    out_specs = P("grp", "row", None, None)
    return jax.shard_map(
        body, mesh=mesh, in_specs=in_specs, out_specs=out_specs, check_vma=False
    )
```

```python
import functools
import math

import jax
import jax.numpy as jnp
import numpy as np
from jax import lax
from jax.experimental import pallas as pl
from jax.experimental.pallas import tpu as pltpu
from jax.sharding import PartitionSpec as P

GROUPS = 32


norm_eps = 1e-06


def extended(cells, sides, width):
    for axis, dim in sides:
        count = lax.axis_size(axis)
        ends = count - 1
        head = lax.slice_in_dim(cells, 0, width, axis=dim)
        tail = lax.slice_in_dim(cells, cells.shape[dim] - width, cells.shape[dim], axis=dim)
        cells = jnp.concatenate(
            [
                lax.ppermute(tail, axis, [(i, (i + 1) % count) for i in range(ends)]),
                cells,
                lax.ppermute(head, axis, [((i + 1) % count, i) for i in range(ends)]),
            ],
            axis=dim,
        )
    return cells


def pad_field(rimmed):
    spaced = jnp.pad(rimmed, ((0, 0), (0, 0), (1, 1), (0, 0)))
    first_frame = spaced[:1]
    return jnp.concatenate([first_frame, first_frame, spaced], axis=0)


def tap_windows(padded, frame_count, row_count, col_count):
    windows = []
    for frame_tap in range(3):
        for row_tap in range(3):
            for col_tap in range(3):
                windows.append(
                    padded[
                        frame_tap : frame_tap + frame_count,
                        row_tap : row_tap + row_count,
                        col_tap : col_tap + col_count,
                    ]
                )
    stacked = jnp.stack(windows, axis=3)
    return stacked.reshape(frame_count * row_count * col_count, -1)


def tap_products(padded, weight, frame_count, row_count, col_count):
    running = jnp.zeros((frame_count * row_count * col_count, weight.shape[2]), jnp.float32)
    for frame_tap in range(3):
        for row_tap in range(3):
            for col_tap in range(3):
                tap_index = (frame_tap * 3 + row_tap) * 3 + col_tap
                window = padded[
                    frame_tap : frame_tap + frame_count,
                    row_tap : row_tap + row_count,
                    col_tap : col_tap + col_count,
                ]
                window = window.reshape(frame_count * row_count * col_count, -1)
                running = running + jnp.dot(
                    window, weight[tap_index], preferred_element_type=jnp.float32
                )
    return running


def group_norm(volume, gain):
    grouped = volume.astype(jnp.float32).reshape(volume.shape[:3] + (GROUPS, -1))
    entry_count = (
        volume.shape[0]
        * volume.shape[1]
        * lax.axis_size("row")
        * volume.shape[2]
        * grouped.shape[4]
    )
    group_total = lax.psum(jnp.sum(grouped, axis=(0, 1, 2, 4)), "row")
    group_avg = group_total / entry_count
    centred = grouped - group_avg[:, None]
    variance = lax.psum(jnp.sum(centred * centred, axis=(0, 1, 2, 4)), "row") / entry_count
    normal_part = centred * lax.rsqrt(variance + norm_eps)[:, None]
    return normal_part.reshape(volume.shape) * gain


def per_device(latent, w_in, gain_in, w_query, w_key, w_value, w_out, gain_up, w_up):
    frame_count, row_count, col_count, _ = latent.shape
    chan_width = w_query.shape[0]
    rimmed = extended(latent, (("row", 1),), 1)
    first_out = jnp.dot(
        tap_windows(pad_field(rimmed), frame_count, row_count, col_count),
        w_in.reshape(-1, chan_width),
        preferred_element_type=jnp.float32,
    )
    first_out = first_out.astype(jnp.bfloat16).reshape(
        frame_count, row_count, col_count, chan_width
    )
    normed = group_norm(first_out, gain_in).astype(jnp.bfloat16)
    flat_rows = normed.reshape(-1, chan_width)
    queries = jnp.dot(flat_rows, w_query, preferred_element_type=jnp.float32).astype(jnp.bfloat16)
    queries = queries.reshape(frame_count, row_count * col_count, chan_width)
    score_scale = 1.0 / math.sqrt(chan_width)
    key_table = jnp.dot(flat_rows, w_key, preferred_element_type=jnp.float32).astype(jnp.bfloat16)
    value_table = jnp.dot(flat_rows, w_value, preferred_element_type=jnp.float32).astype(
        jnp.bfloat16
    )
    key_table = key_table.reshape(frame_count, row_count, col_count, chan_width)
    value_table = value_table.reshape(frame_count, row_count, col_count, chan_width)
    row_peak = jnp.full((frame_count, row_count * col_count), -jnp.inf, jnp.float32)
    denom = jnp.zeros((frame_count, row_count * col_count), jnp.float32)
    weighted = jnp.zeros((frame_count, row_count * col_count, chan_width), jnp.float32)
    scores = (
        jnp.einsum(
            "fqd,fkd->fqk",
            queries,
            lax.all_gather(key_table, "row", axis=1, tiled=True).reshape(
                frame_count, -1, chan_width
            ),
            preferred_element_type=jnp.float32,
        )
        * score_scale
    )
    new_peak = jnp.max(scores, axis=-1)
    correction = jnp.exp(row_peak - new_peak)
    expo = jnp.exp(scores - new_peak[..., None])
    denom = denom * correction + jnp.sum(expo, axis=-1)
    weighted = weighted * correction[..., None] + jnp.einsum(
        "fqk,fkd->fqd",
        expo.astype(jnp.bfloat16),
        lax.all_gather(value_table, "row", axis=1, tiled=True).reshape(frame_count, -1, chan_width),
        preferred_element_type=jnp.float32,
    )
    row_peak, denom, weighted = (new_peak, denom, weighted)
    attended = (weighted / denom[..., None]).astype(jnp.bfloat16).reshape(-1, chan_width)
    added = first_out.astype(jnp.float32).reshape(-1, chan_width) + jnp.dot(
        attended, w_out, preferred_element_type=jnp.float32
    )
    added = added.astype(jnp.bfloat16).reshape(frame_count, row_count, col_count, chan_width)
    full_up = lax.all_gather(w_up, "row", axis=1, tiled=True)
    upsampled = jnp.repeat(jnp.repeat(added, 2, axis=1), 2, axis=2)
    up_rimmed = extended(upsampled, (("row", 1),), 1)
    padded_up = pad_field(up_rimmed)
    running = tap_products(padded_up, full_up, frame_count, 2 * row_count, 2 * col_count)
    convolved = running.astype(jnp.bfloat16).reshape(
        frame_count, 2 * row_count, 2 * col_count, chan_width
    )
    return jax.nn.silu(group_norm(convolved, gain_up)).astype(jnp.bfloat16)


LANES = 128
MIB = 1024 * 1024


def lane_iota(width):
    return lax.broadcasted_iota(jnp.int32, (1, width), 1)


def swap_blocks(arrays, width):
    arrays = list(arrays)
    block = lane_iota(LANES) // width
    step = 1
    while step < len(arrays):
        low = (block & step) == 0
        for t in range(len(arrays)):
            if t & step == 0:
                a, b = arrays[t], arrays[t | step]
                arrays[t] = jnp.where(low, a, pltpu.roll(b, step * width, 1))
                arrays[t | step] = jnp.where(low, pltpu.roll(a, LANES - step * width, 1), b)
        step *= 2
    return arrays


def group_sum(row, group):
    width = row.shape[1]
    lane = lane_iota(width)
    step = 1
    while step < group:
        low = (lane & step) == 0
        row = row + jnp.where(
            low, pltpu.roll(row, width - step, 1), pltpu.roll(row, step, 1)
        )
        step *= 2
    return row


def fold_rows(block):
    return jnp.sum(block.reshape(-1, 8, block.shape[1]), axis=0)


def all_rows(part):
    return jnp.broadcast_to(jnp.sum(part, axis=0, keepdims=True), part.shape)


def pack_kernel(w_any, out_any, w_ref, out_ref, sems, out_sems):
    taps, _, chan_width = w_any.shape
    groups, devices = out_ref.shape[:2]
    share = chan_width // devices
    blocks = LANES // share
    copies, outs = [], []
    for g in range(groups):
        at = slice(g * blocks, min((g + 1) * blocks, taps))
        copies.append(pltpu.make_async_copy(w_any.at[at], w_ref.at[at], sems.at[g]))
        copies[-1].start()
    for g in range(groups):
        copies[g].wait()
        for col in range(chan_width // LANES):
            pieces = []
            for k in range(blocks):
                tap = g * blocks + k
                if tap < taps:
                    pieces.append(
                        w_ref[tap, :, col * LANES : (col + 1) * LANES].astype(jnp.float32)
                    )
                else:
                    pieces.append(jnp.zeros_like(pieces[0]))
            for d, piece in enumerate(swap_blocks(pieces, share)):
                out_ref[g, col * blocks + d] = piece.astype(out_ref.dtype)
        outs.append(
            pltpu.make_async_copy(
                out_ref.at[g], out_any.at[:, :, g * LANES : (g + 1) * LANES], out_sems.at[g]
            )
        )
        outs[-1].start()
    for copy in outs:
        copy.wait()


def mid_kernel(
    dims, near_ref, far_ref, spread_ref, w_in_ref, gain_ref, wq_ref, wk_ref, wv_ref, wo_ref, out_ref,
    x32, wide, edge, h_ref, q_ref, k_ref, v_ref,
):
    frames, rows, own, cols, zc, chan, chunk = dims
    per_frame = rows * cols
    total = frames * per_frame
    step = per_frame // 2
    per_tile = LANES // zc
    block = lane_iota(LANES) // zc
    me = lax.axis_index("row")
    order = rounds(rows // own)

    def piece(row, at):
        differs = me ^ (row // own)
        place = sum(
            ((differs >> (bit.bit_length() - 1)) & 1) << r for r, bit in enumerate(order[:-1])
        )
        return jnp.where(differs & order[-1] == 0, near_ref[place, at, :], far_ref[place, at, :])

    for f in range(frames):
        for g in range(rows // per_tile):
            tile = jnp.concatenate(
                [piece(g * per_tile + i, slice(f * zc, (f + 1) * zc)) for i in range(per_tile)], 0
            ).astype(jnp.float32)
            turned = tile.T
            for i in range(per_tile):
                at = f * per_frame + (g * per_tile + i) * cols
                x32[at : at + cols, :] = jnp.where(block == i, turned, 0.0).astype(x32.dtype)

    lane = lane_iota(edge.shape[2])
    col_tap = (lane // zc) % 3
    row_tap = (lane // zc) // 3
    blank = jnp.zeros((cols, edge.shape[2]), jnp.float32)
    col_index = lax.broadcasted_iota(jnp.int32, (cols, 1), 0)

    for f in range(frames):
        edge[f, 0:cols, :] = blank
        edge[f, (rows + 1) * cols : (rows + 2) * cols, :] = blank

        def columns(c, _):
            at = pl.multiple_of(f * per_frame + c * step, 16)
            v = jnp.dot(
                x32[pl.ds(at, step), :], spread_ref[...], preferred_element_type=jnp.float32
            )
            for k in range(step // cols):
                u = v[k * cols : (k + 1) * cols]
                before = jnp.where(col_index == 0, 0.0, pltpu.roll(u, 1, 0))
                after = jnp.where(col_index == cols - 1, 0.0, pltpu.roll(u, cols - 1, 0))
                u = jnp.where(col_tap == 0, before, jnp.where(col_tap == 2, after, u))
                edge[f, pl.ds(pl.multiple_of(c * step + (k + 1) * cols, 8), cols), :] = u
            return 0

        lax.fori_loop(0, per_frame // step, columns, 0)

        def lines(i, _):
            at = pl.multiple_of(i * cols, 8)
            above = edge[f, pl.ds(at, cols), :]
            here = edge[f, pl.ds(pl.multiple_of(at + cols, 8), cols), :]
            below = edge[f, pl.ds(pl.multiple_of(at + 2 * cols, 8), cols), :]
            v = jnp.where(row_tap == 0, above, jnp.where(row_tap == 2, below, here))
            wide[pl.ds(pl.multiple_of(f * per_frame + at, 16), cols), :] = v.astype(wide.dtype)
            return 0

        lax.fori_loop(0, rows, lines, 0, unroll=2)

    depth = wide.shape[1]

    def first(c, part):
        for f in range(frames):
            acc = None
            for dt in range(3):
                source = max(f + dt - 2, 0)
                at = pl.multiple_of(source * per_frame + c * chunk, 16)
                term = jnp.dot(
                    wide[pl.ds(at, chunk), :],
                    w_in_ref[dt * depth : (dt + 1) * depth, :],
                    preferred_element_type=jnp.float32,
                )
                acc = term if acc is None else acc + term
            acc = acc.astype(jnp.bfloat16)
            h_ref[pl.ds(pl.multiple_of(f * per_frame + c * chunk, 16), chunk), :] = acc
            part = part + fold_rows(acc.astype(jnp.float32))
        return part

    zero = jnp.zeros((8, chan), jnp.float32)
    part = lax.fori_loop(0, per_frame // chunk, first, zero)
    group = chan // GROUPS
    count = total * group
    mean = group_sum(all_rows(part), group) / count
    mean_row = mean[0:1]

    def spreadness(c, part):
        v = h_ref[pl.ds(pl.multiple_of(c * chunk, 16), chunk), :].astype(jnp.float32) - mean_row
        return part + fold_rows(v * v)

    part = lax.fori_loop(0, total // chunk, spreadness, zero)
    variance = group_sum(all_rows(part), group) / count
    scale_row = lax.rsqrt(variance + norm_eps)[0:1]
    gain_row = gain_ref[...]

    def project(c, _):
        at = pl.ds(pl.multiple_of(c * chunk, 16), chunk)
        v = h_ref[at, :].astype(jnp.float32) - mean_row
        normed = (v * scale_row * gain_row).astype(jnp.bfloat16)
        for w, o in ((wq_ref, q_ref), (wk_ref, k_ref), (wv_ref, v_ref)):
            o[at, :] = jnp.dot(normed, w[...], preferred_element_type=jnp.float32).astype(
                jnp.bfloat16
            )
        return 0

    lax.fori_loop(0, total // chunk, project, 0)
    score_scale = 1.0 / math.sqrt(chan)

    def attend(c, _):
        for f in range(frames):
            at = pl.ds(pl.multiple_of(f * per_frame + c * chunk, 16), chunk)
            span = slice(f * per_frame, (f + 1) * per_frame)
            scores = lax.dot_general(
                q_ref[at, :],
                k_ref[span, :],
                (((1,), (1,)), ((), ())),
                preferred_element_type=jnp.float32,
            )
            peak = jnp.max(scores, axis=-1, keepdims=True)
            expo = jnp.exp((scores - peak) * score_scale)
            denom = jnp.sum(expo, axis=-1, keepdims=True)
            mixed = jnp.dot(
                expo.astype(jnp.bfloat16), v_ref[span, :], preferred_element_type=jnp.float32
            )
            mixed = (mixed * (1.0 / denom)).astype(jnp.bfloat16)
            shifted = jnp.dot(mixed, wo_ref[...], preferred_element_type=jnp.float32)
            out_ref[at, :] = (h_ref[at, :].astype(jnp.float32) + shifted).astype(jnp.bfloat16)
        return 0

    lax.fori_loop(0, per_frame // chunk, attend, 0)


def up_kernel(
    dims, w_ref, x_ref, gain_ref, out_ref,
    fold_all, fold_old, fold_new, t_ref, m0_ref, m2_ref, s_old_ref, s_new_ref,
):
    frames, rows, cols, chan, share, chunk = dims
    per_frame = rows * cols
    width = 4 * share
    old_end, new_start = s_old_ref.shape[0], w_ref.shape[1] - s_new_ref.shape[0]
    lane = lane_iota(4 * width)
    phase, shift = (lane // share) % 4, lane // width
    same = lax.broadcasted_iota(jnp.int32, (share, 4 * width), 0) == lane % share
    p, q = phase // 2, phase % 2
    s_old_ref[18 * share :, :] = jnp.zeros((old_end - 18 * share, 4 * width), jnp.bfloat16)
    s_new_ref[: 18 * share - new_start, :] = jnp.zeros(
        (18 * share - new_start, 4 * width), jnp.bfloat16
    )
    spare = s_new_ref.shape[0] + new_start - 27 * share
    s_new_ref[27 * share - new_start :, :] = jnp.zeros((spare, 4 * width), jnp.bfloat16)
    for di in range(3):
        for dj in range(3):
            down = (di == 2) & (p == 1) | (di == 0) & (p == 0)
            along = (dj == 2) & (q == 1) | (dj == 0) & (q == 0)
            wanted = 2 * down.astype(jnp.int32) + along.astype(jnp.int32)
            value = jnp.where(same & (shift == wanted), 1.0, 0.0).astype(jnp.bfloat16)
            tap = (3 * di + dj) * share
            s_old_ref[tap : tap + share, :] = value
            s_old_ref[9 * share + tap : 9 * share + tap + share, :] = value
            tap += 18 * share - new_start
            s_new_ref[tap : tap + share, :] = value
    for c in range(chan // chunk):
        at = slice(c * chunk, (c + 1) * chunk)
        old = jnp.dot(w_ref[at, :old_end], s_old_ref[...], preferred_element_type=jnp.float32)
        new = jnp.dot(w_ref[at, new_start:], s_new_ref[...], preferred_element_type=jnp.float32)
        fold_old[at, :] = old.astype(jnp.bfloat16)
        fold_new[at, :] = new.astype(jnp.bfloat16)
        fold_all[at, :] = (old + new).astype(jnp.bfloat16)

    def products(c, _):
        at0 = pl.ds(pl.multiple_of(c * chunk, 16), chunk)
        at1 = pl.ds(pl.multiple_of(per_frame + c * chunk, 16), chunk)
        t_ref[at0, :] = jnp.dot(x_ref[at0, :], fold_all[...], preferred_element_type=jnp.float32)
        t_ref[at1, :] = jnp.dot(
            x_ref[at0, :], fold_old[...], preferred_element_type=jnp.float32
        ) + jnp.dot(x_ref[at1, :], fold_new[...], preferred_element_type=jnp.float32)
        return 0

    lax.fori_loop(0, per_frame // chunk, products, 0)
    lane = lane_iota(width)
    right = (lane // share) % 2 == 1
    lower = (lane // share) // 2 == 1
    col_index = lax.broadcasted_iota(jnp.int32, (cols, 1), 0)

    def beside(v):
        before = jnp.where(col_index == 0, 0.0, pltpu.roll(v, 1, 0))
        after = jnp.where(col_index == cols - 1, 0.0, pltpu.roll(v, cols - 1, 0))
        return jnp.where(right, after, before)

    blank = jnp.zeros((cols, width), jnp.float32)
    part = jnp.zeros((8, width), jnp.float32)
    for f in range(frames):
        m2_ref[f, 0:cols, :] = blank
        m2_ref[f, (rows + 1) * cols : (rows + 2) * cols, :] = blank

        def columns(i, _):
            at = pl.ds(pl.multiple_of(f * per_frame + i * cols, 8), cols)
            m0_ref[at, :] = t_ref[at, 0:width] + beside(t_ref[at, width : 2 * width])
            m2_ref[f, pl.ds(pl.multiple_of((i + 1) * cols, 8), cols), :] = t_ref[
                at, 2 * width : 3 * width
            ] + beside(t_ref[at, 3 * width : 4 * width])
            return 0

        lax.fori_loop(0, rows, columns, 0, unroll=2)

        def lines(i, part):
            at = pl.ds(pl.multiple_of(f * per_frame + i * cols, 8), cols)
            above = m2_ref[f, pl.ds(pl.multiple_of(i * cols, 8), cols), :]
            below = m2_ref[f, pl.ds(pl.multiple_of((i + 2) * cols, 8), cols), :]
            v = m0_ref[at, :] + jnp.where(lower, below, above)
            v = v.astype(jnp.bfloat16).astype(jnp.float32)
            m0_ref[at, :] = v
            return part + fold_rows(v)

        part = lax.fori_loop(0, rows, lines, part, unroll=2)

    group = chan // GROUPS
    count = frames * rows * cols * 4 * group

    def grouped(part):
        part = all_rows(part)
        part = part + pltpu.roll(part, 2 * share, 1)
        part = part + pltpu.roll(part, share, 1)
        return group_sum(part, group)

    mean_row = (grouped(part) / count)[0:1]

    def spreadness(i, part):
        v = m0_ref[pl.ds(pl.multiple_of(i * cols, 8), cols), :] - mean_row
        return part + fold_rows(v * v)

    part = lax.fori_loop(
        0, frames * rows, spreadness, jnp.zeros((8, width), jnp.float32), unroll=2
    )
    variance = grouped(part) / count
    me = lax.axis_index("row")
    gains = jnp.broadcast_to(gain_ref[...], (8, chan))
    gains = jnp.where(lane_iota(chan) // share == me, gains, 0.0)
    gains = sum(gains[:, k : k + width] for k in range(0, chan, width))
    gains = gains + pltpu.roll(gains, 2 * share, 1)
    gains = gains + pltpu.roll(gains, share, 1)
    scale_row = (lax.rsqrt(variance + norm_eps) * gains)[0:1]

    devices = out_ref.shape[0]
    own = rows // devices

    def finish(d, _):
        for f in range(frames):
            for r in range(own):
                at = pl.ds(pl.multiple_of(f * per_frame + (d * own + r) * cols, 8), cols)
                v = (m0_ref[at, :] - mean_row) * scale_row
                v = v / (1.0 + jnp.exp(-v))
                out_ref[d, (f * own + r) * cols : (f * own + r + 1) * cols, :] = v.astype(
                    out_ref.dtype
                )
        return 0

    lax.fori_loop(0, devices, finish, 0, unroll=2)


def place_kernel(share, x_ref, out_ref, line):
    devices = x_ref.shape[0]
    frames, lines, wide_cols, _ = out_ref.shape
    cols = wide_cols // 2
    own = lines // 2
    blocks = LANES // share
    for a in range(devices // blocks):
        for f in range(frames):
            for r in range(own):
                at = slice((f * own + r) * cols, (f * own + r + 1) * cols)
                pieces = swap_blocks(
                    [x_ref[a * blocks + s, at, :].astype(jnp.float32) for s in range(blocks)],
                    share,
                )
                for p in range(2):
                    slot = ((a * frames + f) * own + r) * 2 + p
                    for q in range(2):
                        line[slot, pl.ds(q, cols, stride=2), :] = pieces[2 * p + q]
                    out_ref[f, 2 * r + p, :, a * LANES : (a + 1) * LANES] = line[slot].astype(
                        out_ref.dtype
                    )


def fits(mesh, shapes):
    latent, w_query = shapes
    count = mesh.shape["row"]
    frames, own, cols, zc = latent
    chan = w_query[0]
    rows = own * count
    return (
        frames == 2
        and own == 1
        and count & (count - 1) == 0
        and chan == count * 32
        and LANES % zc == 0
        and LANES // zc == 8
        and cols % 16 == 0
        and cols <= LANES
        and rows % 8 == 0
        and (rows * cols) % 256 == 0
        and rows * cols <= 1024
    )


def call(kernel, out_shape, scratch, limit, flops, moved, spaces, out_space=pltpu.VMEM):
    return pl.pallas_call(
        kernel,
        out_shape=out_shape,
        in_specs=[pl.BlockSpec(memory_space=space) for space in spaces],
        out_specs=pl.BlockSpec(memory_space=out_space),
        scratch_shapes=scratch,
        compiler_params=pltpu.CompilerParams(vmem_limit_bytes=limit * MIB),
        cost_estimate=pl.CostEstimate(flops=flops, bytes_accessed=moved, transcendentals=0),
    )


def rounds(count):
    bits = [1]
    bit = count // 2
    while bit > 1:
        bits.append(bit)
        bit //= 2
    return bits


def everyone(cells, held):
    count = lax.axis_size("row")
    me = lax.axis_index("row")
    sent = cells[None]
    cells = lax.optimization_barrier(jnp.where(me < count, sent, 0))
    order = rounds(count)
    for bit in order:
        pairs = [(k, k ^ bit) for k in range(count)]
        if bit == order[-1]:
            cells, held = lax.optimization_barrier((cells, held))
            return cells, lax.ppermute(cells, "row", pairs), held
        other = lax.ppermute(sent, "row", pairs)
        cells = sent = jnp.concatenate([cells, other], 0)


def whole_video(latent, w_in, gain_in, w_query, w_key, w_value, w_out, gain_up, w_up):
    frames, own, cols, zc = latent.shape
    chan = w_query.shape[0]
    count = lax.axis_size("row")
    rows = own * count
    positions = frames * rows * cols
    share = chan // count
    blocks = LANES // share
    pad_taps = -(-27 // blocks) * blocks
    f32, bf16 = jnp.float32, jnp.bfloat16
    shape = jax.ShapeDtypeStruct
    chunk = 256

    cells = jnp.swapaxes(latent, 2, 3).reshape(frames * zc, cols)

    packed = call(
        pack_kernel, shape((count, w_up.shape[1], pad_taps * share), bf16),
        [
            pltpu.VMEM((pad_taps,) + w_up.shape[1:], bf16),
            pltpu.VMEM((pad_taps // blocks, count, w_up.shape[1], LANES), bf16),
            pltpu.SemaphoreType.DMA((pad_taps // blocks,)),
            pltpu.SemaphoreType.DMA((pad_taps // blocks,)),
        ],
        60,
        10**6,
        2 * 10**6,
        (pltpu.HBM,),
        pltpu.HBM,
    )(w_up)
    near, far, packed = everyone(cells, packed)
    weights = lax.all_to_all(packed, "row", 0, 0, tiled=True)
    weights = weights.reshape(chan, pad_taps * share)

    depth = 9 * zc
    spread = np.zeros((LANES, depth), np.float32)
    for k in range(LANES):
        for t in range(9):
            spread[k, t * zc + k % zc] = 1.0
    dims = (frames, rows, own, cols, zc, chan, chunk)
    added = call(
        functools.partial(mid_kernel, dims),
        shape((positions, chan), bf16),
        [
            pltpu.VMEM((positions, LANES), bf16),
            pltpu.VMEM((positions, depth), bf16),
            pltpu.VMEM((frames, (rows + 2) * cols, depth), f32),
        ]
        + [pltpu.VMEM((positions, chan), bf16)] * 4,
        28,
        7 * 10**9,
        6 * 10**6,
        (pltpu.VMEM,) * 9,
    )(
        near,
        far,
        jnp.asarray(spread, bf16),
        w_in.reshape(3 * depth, chan),
        gain_in.reshape(1, chan),
        w_query,
        w_key,
        w_value,
        w_out,
    )

    old_end = -(-18 * share // LANES) * LANES
    new_start = 18 * share // LANES * LANES
    dims = (frames, rows, cols, chan, share, chunk)
    width = 4 * share
    decoded = call(
        functools.partial(up_kernel, dims),
        shape((count, frames * own * cols, width), bf16),
        [pltpu.VMEM((chan, 4 * width), bf16)] * 3
        + [
            pltpu.VMEM((positions, 4 * width), f32),
            pltpu.VMEM((positions, width), f32),
            pltpu.VMEM((frames, (rows + 2) * cols, width), f32),
            pltpu.VMEM((old_end, 4 * width), bf16),
            pltpu.VMEM((pad_taps * share - new_start, 4 * width), bf16),
        ],
        16,
        3 * 10**9,
        5 * 10**6,
        (pltpu.VMEM,) * 3,
    )(weights, added, gain_up.reshape(1, chan))
    swapped = lax.all_to_all(decoded, "row", 0, 0, tiled=True)
    slots = (count // blocks) * frames * own * 2
    return call(
        functools.partial(place_kernel, share),
        shape((frames, 2 * own, 2 * cols, chan), bf16),
        [pltpu.VMEM((slots, 2 * cols, LANES), f32)],
        8,
        10**6,
        10**6,
        (pltpu.VMEM,),
    )(swapped)


def solution(mesh):
    def body(*args):
        whole = fits(mesh, (args[0].shape, args[3].shape))
        return (whole_video if whole else per_device)(*args)

    in_specs = (
        P("grp", "row", None, None),
        P(),
        P(),
        P(),
        P(),
        P(),
        P(),
        P(),
        P(None, "row", None),
    )
    out_specs = P("grp", "row", None, None)
    return jax.shard_map(
        body, mesh=mesh, in_specs=in_specs, out_specs=out_specs, check_vma=False
    )
```

```python
import functools
import math

import jax
import jax.numpy as jnp
import numpy as np
from jax import lax
from jax.experimental import pallas as pl
from jax.experimental.pallas import tpu as pltpu
from jax.sharding import PartitionSpec as P

GROUPS = 32


norm_eps = 1e-06


def extended(cells, sides, width):
    for axis, dim in sides:
        count = lax.axis_size(axis)
        ends = count - 1
        head = lax.slice_in_dim(cells, 0, width, axis=dim)
        tail = lax.slice_in_dim(cells, cells.shape[dim] - width, cells.shape[dim], axis=dim)
        cells = jnp.concatenate(
            [
                lax.ppermute(tail, axis, [(i, (i + 1) % count) for i in range(ends)]),
                cells,
                lax.ppermute(head, axis, [((i + 1) % count, i) for i in range(ends)]),
            ],
            axis=dim,
        )
    return cells


def pad_field(rimmed):
    spaced = jnp.pad(rimmed, ((0, 0), (0, 0), (1, 1), (0, 0)))
    first_frame = spaced[:1]
    return jnp.concatenate([first_frame, first_frame, spaced], axis=0)


def tap_windows(padded, frame_count, row_count, col_count):
    windows = []
    for frame_tap in range(3):
        for row_tap in range(3):
            for col_tap in range(3):
                windows.append(
                    padded[
                        frame_tap : frame_tap + frame_count,
                        row_tap : row_tap + row_count,
                        col_tap : col_tap + col_count,
                    ]
                )
    stacked = jnp.stack(windows, axis=3)
    return stacked.reshape(frame_count * row_count * col_count, -1)


def tap_products(padded, weight, frame_count, row_count, col_count):
    running = jnp.zeros((frame_count * row_count * col_count, weight.shape[2]), jnp.float32)
    for frame_tap in range(3):
        for row_tap in range(3):
            for col_tap in range(3):
                tap_index = (frame_tap * 3 + row_tap) * 3 + col_tap
                window = padded[
                    frame_tap : frame_tap + frame_count,
                    row_tap : row_tap + row_count,
                    col_tap : col_tap + col_count,
                ]
                window = window.reshape(frame_count * row_count * col_count, -1)
                running = running + jnp.dot(
                    window, weight[tap_index], preferred_element_type=jnp.float32
                )
    return running


def group_norm(volume, gain):
    grouped = volume.astype(jnp.float32).reshape(volume.shape[:3] + (GROUPS, -1))
    entry_count = (
        volume.shape[0]
        * volume.shape[1]
        * lax.axis_size("row")
        * volume.shape[2]
        * grouped.shape[4]
    )
    group_total = lax.psum(jnp.sum(grouped, axis=(0, 1, 2, 4)), "row")
    group_avg = group_total / entry_count
    centred = grouped - group_avg[:, None]
    variance = lax.psum(jnp.sum(centred * centred, axis=(0, 1, 2, 4)), "row") / entry_count
    normal_part = centred * lax.rsqrt(variance + norm_eps)[:, None]
    return normal_part.reshape(volume.shape) * gain


def per_device(latent, w_in, gain_in, w_query, w_key, w_value, w_out, gain_up, w_up):
    frame_count, row_count, col_count, _ = latent.shape
    chan_width = w_query.shape[0]
    rimmed = extended(latent, (("row", 1),), 1)
    first_out = jnp.dot(
        tap_windows(pad_field(rimmed), frame_count, row_count, col_count),
        w_in.reshape(-1, chan_width),
        preferred_element_type=jnp.float32,
    )
    first_out = first_out.astype(jnp.bfloat16).reshape(
        frame_count, row_count, col_count, chan_width
    )
    normed = group_norm(first_out, gain_in).astype(jnp.bfloat16)
    flat_rows = normed.reshape(-1, chan_width)
    queries = jnp.dot(flat_rows, w_query, preferred_element_type=jnp.float32).astype(jnp.bfloat16)
    queries = queries.reshape(frame_count, row_count * col_count, chan_width)
    score_scale = 1.0 / math.sqrt(chan_width)
    key_table = jnp.dot(flat_rows, w_key, preferred_element_type=jnp.float32).astype(jnp.bfloat16)
    value_table = jnp.dot(flat_rows, w_value, preferred_element_type=jnp.float32).astype(
        jnp.bfloat16
    )
    key_table = key_table.reshape(frame_count, row_count, col_count, chan_width)
    value_table = value_table.reshape(frame_count, row_count, col_count, chan_width)
    row_peak = jnp.full((frame_count, row_count * col_count), -jnp.inf, jnp.float32)
    denom = jnp.zeros((frame_count, row_count * col_count), jnp.float32)
    weighted = jnp.zeros((frame_count, row_count * col_count, chan_width), jnp.float32)
    scores = (
        jnp.einsum(
            "fqd,fkd->fqk",
            queries,
            lax.all_gather(key_table, "row", axis=1, tiled=True).reshape(
                frame_count, -1, chan_width
            ),
            preferred_element_type=jnp.float32,
        )
        * score_scale
    )
    new_peak = jnp.max(scores, axis=-1)
    correction = jnp.exp(row_peak - new_peak)
    expo = jnp.exp(scores - new_peak[..., None])
    denom = denom * correction + jnp.sum(expo, axis=-1)
    weighted = weighted * correction[..., None] + jnp.einsum(
        "fqk,fkd->fqd",
        expo.astype(jnp.bfloat16),
        lax.all_gather(value_table, "row", axis=1, tiled=True).reshape(frame_count, -1, chan_width),
        preferred_element_type=jnp.float32,
    )
    row_peak, denom, weighted = (new_peak, denom, weighted)
    attended = (weighted / denom[..., None]).astype(jnp.bfloat16).reshape(-1, chan_width)
    added = first_out.astype(jnp.float32).reshape(-1, chan_width) + jnp.dot(
        attended, w_out, preferred_element_type=jnp.float32
    )
    added = added.astype(jnp.bfloat16).reshape(frame_count, row_count, col_count, chan_width)
    full_up = lax.all_gather(w_up, "row", axis=1, tiled=True)
    upsampled = jnp.repeat(jnp.repeat(added, 2, axis=1), 2, axis=2)
    up_rimmed = extended(upsampled, (("row", 1),), 1)
    padded_up = pad_field(up_rimmed)
    running = tap_products(padded_up, full_up, frame_count, 2 * row_count, 2 * col_count)
    convolved = running.astype(jnp.bfloat16).reshape(
        frame_count, 2 * row_count, 2 * col_count, chan_width
    )
    return jax.nn.silu(group_norm(convolved, gain_up)).astype(jnp.bfloat16)


LANES = 128
MIB = 1024 * 1024


def lane_iota(width):
    return lax.broadcasted_iota(jnp.int32, (1, width), 1)


def swap_blocks(arrays, width):
    arrays = list(arrays)
    block = lane_iota(LANES) // width
    step = 1
    while step < len(arrays):
        low = (block & step) == 0
        for t in range(len(arrays)):
            if t & step == 0:
                a, b = arrays[t], arrays[t | step]
                arrays[t] = jnp.where(low, a, pltpu.roll(b, step * width, 1))
                arrays[t | step] = jnp.where(low, pltpu.roll(a, LANES - step * width, 1), b)
        step *= 2
    return arrays


def group_sum(row, group):
    width = row.shape[1]
    lane = lane_iota(width)
    step = 1
    while step < group:
        low = (lane & step) == 0
        row = row + jnp.where(
            low, pltpu.roll(row, width - step, 1), pltpu.roll(row, step, 1)
        )
        step *= 2
    return row


def fold_rows(block):
    return jnp.sum(block.reshape(-1, 8, block.shape[1]), axis=0)


def all_rows(part):
    return jnp.broadcast_to(jnp.sum(part, axis=0, keepdims=True), part.shape)


def tap_tiles(taps, blocks):
    whole, rest = taps // blocks, taps % blocks
    tiles = [[(h, t * blocks + k) for k in range(blocks)] for h in range(2) for t in range(whole)]
    tail = []
    for h in range(2):
        tail += [(h, whole * blocks + k) for k in range(rest)]
        tail += [None] * (blocks // 2 - rest)
    return tiles + [tail]


def pack_kernel(w_any, out_any, w_ref, out_ref, sems, out_sems):
    taps, _, width = w_ref.shape
    groups, devices, depth, _ = out_ref.shape
    share = width // devices
    blocks = LANES // share
    first = pl.multiple_of(lax.axis_index("grp") * width, LANES)
    copies, outs = [], []
    for g in range(sems.shape[0]):
        at = slice(g * blocks, min((g + 1) * blocks, taps))
        copies.append(
            pltpu.make_async_copy(
                w_any.at[at, :, pl.ds(first, width)], w_ref.at[at], sems.at[g]
            )
        )
        copies[-1].start()
    tiles = tap_tiles(taps, blocks)
    loaded = 0
    for g in sorted(range(groups), key=lambda g: max(unit[1] for unit in tiles[g] if unit)):
        while loaded * blocks <= max(unit[1] for unit in tiles[g] if unit):
            copies[loaded].wait()
            loaded += 1
        for col in range(width // LANES):
            pieces = [
                jnp.zeros((depth, LANES), jnp.float32)
                if unit is None
                else w_ref[
                    unit[1],
                    unit[0] * depth : (unit[0] + 1) * depth,
                    col * LANES : (col + 1) * LANES,
                ].astype(jnp.float32)
                for unit in tiles[g]
            ]
            for d, piece in enumerate(swap_blocks(pieces, share)):
                out_ref[g, col * blocks + d] = piece.astype(out_ref.dtype)
        outs.append(
            pltpu.make_async_copy(
                out_ref.at[g], out_any.at[:, :, g * LANES : (g + 1) * LANES], out_sems.at[g]
            )
        )
        outs[-1].start()
    for copy in outs:
        copy.wait()


def mid_kernel(
    dims, near_ref, far_ref, spread_ref, w_in_ref, gain_ref, wq_any, wk_any, wv_any, wo_any, out_ref,
    x32, wide, edge, h_ref, q_ref, k_ref, v_ref, wq_ref, wk_ref, wv_ref, wo_ref, sems,
):
    pairs = ((wq_any, wq_ref), (wk_any, wk_ref), (wv_any, wv_ref), (wo_any, wo_ref))
    loads = [pltpu.make_async_copy(a, b, sems.at[k]) for k, (a, b) in enumerate(pairs)]
    for load in loads:
        load.start()
    frames, rows, own, cols, zc, chan, chunk = dims
    per_frame = rows * cols
    total = frames * per_frame
    step = per_frame // 2
    per_tile = LANES // zc
    block = lane_iota(LANES) // zc
    me = lax.axis_index("row")
    order = rounds(rows // own)

    def piece(row, at):
        differs = me ^ (row // own)
        place = sum(
            ((differs >> (bit.bit_length() - 1)) & 1) << r for r, bit in enumerate(order[:-1])
        )
        return jnp.where(differs & order[-1] == 0, near_ref[place, at, :], far_ref[place, at, :])

    for f in range(frames):
        for g in range(rows // per_tile):
            tile = jnp.concatenate(
                [piece(g * per_tile + i, slice(f * zc, (f + 1) * zc)) for i in range(per_tile)], 0
            ).astype(jnp.float32)
            turned = tile.T
            for i in range(per_tile):
                at = f * per_frame + (g * per_tile + i) * cols
                x32[at : at + cols, :] = jnp.where(block == i, turned, 0.0).astype(x32.dtype)

    lane = lane_iota(edge.shape[2])
    col_tap = (lane // zc) % 3
    row_tap = (lane // zc) // 3
    blank = jnp.zeros((cols, edge.shape[2]), jnp.float32)
    col_index = lax.broadcasted_iota(jnp.int32, (cols, 1), 0)

    for f in range(frames):
        edge[f, 0:cols, :] = blank
        edge[f, (rows + 1) * cols : (rows + 2) * cols, :] = blank

        def columns(c, _):
            at = pl.multiple_of(f * per_frame + c * step, 16)
            v = jnp.dot(
                x32[pl.ds(at, step), :], spread_ref[...], preferred_element_type=jnp.float32
            )
            for k in range(step // cols):
                u = v[k * cols : (k + 1) * cols]
                before = jnp.where(col_index == 0, 0.0, pltpu.roll(u, 1, 0))
                after = jnp.where(col_index == cols - 1, 0.0, pltpu.roll(u, cols - 1, 0))
                u = jnp.where(col_tap == 0, before, jnp.where(col_tap == 2, after, u))
                edge[f, pl.ds(pl.multiple_of(c * step + (k + 1) * cols, 8), cols), :] = u
            return 0

        lax.fori_loop(0, per_frame // step, columns, 0)

        def lines(i, _):
            at = pl.multiple_of(i * cols, 8)
            above = edge[f, pl.ds(at, cols), :]
            here = edge[f, pl.ds(pl.multiple_of(at + cols, 8), cols), :]
            below = edge[f, pl.ds(pl.multiple_of(at + 2 * cols, 8), cols), :]
            v = jnp.where(row_tap == 0, above, jnp.where(row_tap == 2, below, here))
            wide[pl.ds(pl.multiple_of(f * per_frame + at, 16), cols), :] = v.astype(wide.dtype)
            return 0

        lax.fori_loop(0, rows, lines, 0, unroll=2)

    depth = wide.shape[1]

    def first(part):
        for f in range(frames):
            acc = None
            for dt in range(3):
                source = max(f + dt - 2, 0)
                at = source * per_frame
                term = jnp.dot(
                    wide[at : at + per_frame, :],
                    w_in_ref[dt * depth : (dt + 1) * depth, :],
                    preferred_element_type=jnp.float32,
                )
                acc = term if acc is None else acc + term
            acc = acc.astype(jnp.bfloat16)
            h_ref[slice(f * per_frame, (f + 1) * per_frame), :] = acc
            part = part + fold_rows(acc.astype(jnp.float32))
        return part

    zero = jnp.zeros((8, chan), jnp.float32)
    part = first(zero)
    group = chan // GROUPS
    count = total * group
    mean = group_sum(all_rows(part), group) / count
    mean_row = mean[0:1]

    def spreadness(c, part):
        v = h_ref[pl.ds(pl.multiple_of(c * chunk, 16), chunk), :].astype(jnp.float32) - mean_row
        return part + fold_rows(v * v)

    part = lax.fori_loop(0, total // chunk, spreadness, zero)
    variance = group_sum(all_rows(part), group) / count
    scale_row = lax.rsqrt(variance + norm_eps)[0:1]
    gain_row = gain_ref[...]

    for load in loads:
        load.wait()

    def project(c, _):
        at = pl.ds(pl.multiple_of(c * chunk, 16), chunk)
        v = h_ref[at, :].astype(jnp.float32) - mean_row
        normed = (v * scale_row * gain_row).astype(jnp.bfloat16)
        for w, o in ((wq_ref, q_ref), (wk_ref, k_ref), (wv_ref, v_ref)):
            o[at, :] = jnp.dot(normed, w[...], preferred_element_type=jnp.float32).astype(
                jnp.bfloat16
            )
        return 0

    lax.fori_loop(0, total // chunk, project, 0, unroll=total // chunk)
    score_scale = 1.0 / math.sqrt(chan)

    for f in range(frames):
        at = slice(f * per_frame, (f + 1) * per_frame)
        span = slice(f * per_frame, (f + 1) * per_frame)
        scores = lax.dot_general(
            q_ref[at, :],
            k_ref[span, :],
            (((1,), (1,)), ((), ())),
            preferred_element_type=jnp.float32,
        )
        peak = jnp.max(scores, axis=-1, keepdims=True)
        expo = jnp.exp2((scores - peak) * (score_scale * math.log2(math.e)))
        denom = jnp.sum(expo, axis=-1, keepdims=True)
        mixed = jnp.dot(
            expo.astype(jnp.bfloat16), v_ref[span, :], preferred_element_type=jnp.float32
        )
        mixed = (mixed * (1.0 / denom)).astype(jnp.bfloat16)
        shifted = jnp.dot(mixed, wo_ref[...], preferred_element_type=jnp.float32)
        out_ref[at, :] = (h_ref[at, :].astype(jnp.float32) + shifted).astype(jnp.bfloat16)


def fold_taps(w_ref, all_ref, new_ref, s_all, s_new, share):
    blocks = LANES // share
    width = s_all.shape[1]
    whole = 27 // blocks
    lane = lane_iota(width)
    inner, shift = (lane // share) % blocks, lane // LANES
    later, p, q = inner // 4 == 1, (inner // 2) % 2, inner % 2
    same = lax.broadcasted_iota(jnp.int32, (share, width), 0) == lane % share
    s_all[whole * LANES :, :] = jnp.zeros((2 * LANES, width), s_all.dtype)
    s_new[...] = jnp.zeros_like(s_new)
    for di in range(3):
        for dj in range(3):
            down = (di == 2) & (p == 1) | (di == 0) & (p == 0)
            along = (dj == 2) & (q == 1) | (dj == 0) & (q == 0)
            wanted = 2 * down.astype(jnp.int32) + along.astype(jnp.int32)
            fits_here = same & (shift == wanted)
            both, early, late = (
                jnp.where(v, 1.0, 0.0).astype(s_all.dtype)
                for v in (fits_here, fits_here & ~later, fits_here & later)
            )
            for dt in range(3):
                tap = 9 * dt + 3 * di + dj
                if tap < whole * blocks:
                    s_all[tap * share : (tap + 1) * share, :] = early if dt == 2 else both
                    if dt == 2:
                        at = (tap - (whole - 1) * blocks) * share
                        s_new[at : at + share, :] = late
                else:
                    for h in range(2):
                        at = h * (LANES + LANES // 2) + (tap - whole * blocks) * share
                        s_all[whole * LANES + at : whole * LANES + at + share, :] = early
                        s_new[LANES + at : LANES + at + share, :] = late
    tail = slice(2 * whole * LANES, (2 * whole + 1) * LANES)
    for h in range(2):
        main = slice(h * whole * LANES, (h + 1) * whole * LANES)
        last = slice(((h + 1) * whole - 1) * LANES, (h + 1) * whole * LANES)
        side = slice((whole + h) * LANES, (whole + h + 1) * LANES)
        new_side = slice((1 + h) * LANES, (2 + h) * LANES)
        for (lanes, s_ref, rows, side_rows), to_ref in (
            ((main, s_all, slice(0, whole * LANES), side), all_ref),
            ((last, s_new, slice(0, LANES), new_side), new_ref),
        ):
            v = jnp.dot(w_ref[:, lanes], s_ref[rows, :], preferred_element_type=jnp.float32)
            v += jnp.dot(w_ref[:, tail], s_ref[side_rows, :], preferred_element_type=jnp.float32)
            v = v.astype(to_ref.dtype)
            for k in range(v.shape[0] // share):
                at = (2 * k + h) * share
                to_ref[at : at + share, :] = v[k * share : (k + 1) * share]


def up_video(dims, x_ref, all_ref, new_ref, gain_ref, t_ref, m0_ref, m2_ref, store):
    rows, cols, chan, share, _ = dims
    per_frame = rows * cols
    width = LANES

    t_ref[...] = jnp.dot(
        x_ref[0:per_frame, :], all_ref[...], preferred_element_type=jnp.float32
    ) + jnp.dot(
        x_ref[per_frame : 2 * per_frame, :], new_ref[...], preferred_element_type=jnp.float32
    )
    lane = lane_iota(width)
    right = (lane // share) % 2 == 1
    lower = (lane // (2 * share)) % 2 == 1
    col_index = lax.broadcasted_iota(jnp.int32, (cols, 1), 0)

    def beside(v):
        before = jnp.where(col_index == 0, 0.0, pltpu.roll(v, 1, 0))
        after = jnp.where(col_index == cols - 1, 0.0, pltpu.roll(v, cols - 1, 0))
        return jnp.where(right, after, before)

    blank = jnp.zeros((cols, width), jnp.float32)
    m2_ref[0:cols, :] = blank
    m2_ref[(rows + 1) * cols : (rows + 2) * cols, :] = blank

    def columns(i, _):
        at = pl.ds(pl.multiple_of(i * cols, 8), cols)
        m0_ref[at, :] = t_ref[at, 0:width] + beside(t_ref[at, width : 2 * width])
        m2_ref[pl.ds(pl.multiple_of((i + 1) * cols, 8), cols), :] = t_ref[
            at, 2 * width : 3 * width
        ] + beside(t_ref[at, 3 * width : 4 * width])
        return 0

    lax.fori_loop(0, rows, columns, 0, unroll=2)

    def lines(i, part):
        at = pl.ds(pl.multiple_of(i * cols, 8), cols)
        above = m2_ref[at, :]
        below = m2_ref[pl.ds(pl.multiple_of((i + 2) * cols, 8), cols), :]
        v = m0_ref[at, :] + jnp.where(lower, below, above)
        v = v.astype(jnp.bfloat16).astype(jnp.float32)
        m0_ref[at, :] = v
        return part + fold_rows(v)

    part = lax.fori_loop(0, rows, lines, jnp.zeros((8, width), jnp.float32), unroll=2)
    group = chan // GROUPS
    count = 2 * rows * cols * 4 * group

    def over_blocks(row):
        step = share
        while step < width:
            row = row + pltpu.roll(row, step, 1)
            step *= 2
        return row

    def grouped(part):
        return group_sum(over_blocks(all_rows(part)), group)

    mean_row = (grouped(part) / count)[0:1]

    def spreadness(i, part):
        v = m0_ref[pl.ds(pl.multiple_of(i * cols, 8), cols), :] - mean_row
        return part + fold_rows(v * v)

    part = lax.fori_loop(0, rows, spreadness, jnp.zeros((8, width), jnp.float32), unroll=2)
    variance = grouped(part) / count
    me = lax.axis_index("grp") * lax.axis_size("row") + lax.axis_index("row")
    gains = jnp.broadcast_to(gain_ref[...], (8, chan))
    gains = jnp.where(lane_iota(chan) // share == me, gains, 0.0)
    gains = over_blocks(sum(gains[:, k : k + width] for k in range(0, chan, width)))
    scale_row = (lax.rsqrt(variance + norm_eps) * gains)[0:1]

    def finish(d, _):
        at = pl.ds(pl.multiple_of(d * cols, 8), cols)
        v = (m0_ref[at, :] - mean_row) * scale_row
        store(d, v / (1.0 + jnp.exp(-v)))
        return 0

    lax.fori_loop(0, rows, finish, 0, unroll=2)


def near_kernel(
    dims, w_ref, x_ref, gain_ref, out_ref, all_ref, new_ref, t_ref, m0_ref, m2_ref, s_all, s_new
):
    fold_taps(w_ref, all_ref, new_ref, s_all, s_new, dims[3])

    def store(d, v):
        out_ref[d] = v.astype(out_ref.dtype)

    up_video(dims, x_ref, all_ref, new_ref, gain_ref, t_ref, m0_ref, m2_ref, store)


def far_kernel(
    dims, near_ref, x_ref, all_ref, new_ref, gain_ref, out_ref, t_ref, m0_ref, m2_ref
):
    rows = dims[0]
    video = lax.axis_index("row") % 2

    def keep(d, _):
        out_ref[video * rows + d] = near_ref[d]
        return 0

    lax.fori_loop(0, rows, keep, 0, unroll=4)

    def store(d, v):
        out_ref[(1 - video) * rows + d] = v.astype(out_ref.dtype)

    up_video(dims, x_ref, all_ref, new_ref, gain_ref, t_ref, m0_ref, m2_ref, store)


def place_kernel(share, x_ref, out_ref, line):
    devices = x_ref.shape[0]
    blocks = LANES // share
    cols = x_ref.shape[1]
    for a in range(devices // blocks):
        pieces = swap_blocks(
            [x_ref[a * blocks + k].astype(jnp.float32) for k in range(blocks)], share
        )
        for half in range(blocks // 2):
            slot = a * (blocks // 2) + half
            for q in range(2):
                line[slot, pl.ds(q, cols, stride=2), :] = pieces[2 * half + q]
            out_ref[half // 2, half % 2, :, a * LANES : (a + 1) * LANES] = line[slot].astype(
                out_ref.dtype
            )


def fits(mesh, shapes):
    latent, w_query = shapes
    count = mesh.shape["row"]
    frames, own, cols, zc = latent
    chan = w_query[0]
    rows = own * count
    share = chan // (2 * count)
    return (
        mesh.shape["grp"] == 2
        and frames == 2
        and own == 1
        and count >= 8
        and count & (count - 1) == 0
        and share == 16
        and chan == 2 * count * share
        and chan == GROUPS * share
        and zc == 16
        and cols % 16 == 0
        and cols <= LANES
        and (rows * cols) % 256 == 0
        and rows * cols <= 1024
    )


def call(kernel, out_shape, scratch, limit, flops, moved, spaces, out_space=pltpu.VMEM):
    return pl.pallas_call(
        kernel,
        out_shape=out_shape,
        in_specs=[pl.BlockSpec(memory_space=space) for space in spaces],
        out_specs=jax.tree.map(lambda space: pl.BlockSpec(memory_space=space), out_space),
        scratch_shapes=scratch,
        compiler_params=pltpu.CompilerParams(vmem_limit_bytes=limit * MIB),
        cost_estimate=pl.CostEstimate(flops=flops, bytes_accessed=moved, transcendentals=0),
    )


def rounds(count):
    bits = [1]
    bit = count // 2
    while bit > 1:
        bits.append(bit)
        bit //= 2
    return bits


def everyone(cells, held):
    count = lax.axis_size("row")
    me = lax.axis_index("row")
    grp = lax.axis_index("grp")
    sent = cells[None]
    own = lax.optimization_barrier(jnp.where(me < count, sent, 0))
    to_one, to_two = [], []
    for g in range(2):
        for k in range(count):
            here = g * count + k
            if g == k % 2:
                to_one.append((here, (1 - g) * count + k))
            else:
                to_one.append((here, g * count + (k ^ 1)))
                to_two.append((here, (1 - g) * count + (k ^ 1)))
    one = lax.ppermute(sent, ("grp", "row"), to_one)
    two = lax.ppermute(sent, ("grp", "row"), to_two)
    mine = grp == me % 2
    cells = sent = jnp.concatenate([jnp.where(mine, own, one), jnp.where(mine, one, two)], 0)
    order = rounds(count)
    for bit in order[1:]:
        pairs = [(k, k ^ bit) for k in range(count)]
        if bit == order[-1]:
            cells, held = lax.optimization_barrier((cells, held))
            return cells, lax.ppermute(cells, "row", pairs), held
        other = lax.ppermute(sent, "row", pairs)
        cells = sent = jnp.concatenate([cells, other], 0)


def whole_video(latent, w_in, gain_in, w_query, w_key, w_value, w_out, gain_up, w_up):
    frames, own, cols, zc = latent.shape
    chan = w_query.shape[0]
    count = lax.axis_size("row")
    rows = own * count
    positions = frames * rows * cols
    share = chan // (2 * count)
    blocks = LANES // share
    tiles = len(tap_tiles(27, blocks))
    f32, bf16 = jnp.float32, jnp.bfloat16
    shape = jax.ShapeDtypeStruct
    chunk = 256

    cells = jnp.swapaxes(latent, 2, 3).reshape(frames * zc, cols)

    packed = call(
        pack_kernel,
        shape((count, share, tiles * LANES), bf16),
        [
            pltpu.VMEM((27, 2 * share, count * share), bf16),
            pltpu.VMEM((tiles, count, share, LANES), bf16),
            pltpu.SemaphoreType.DMA((-(-27 // blocks),)),
            pltpu.SemaphoreType.DMA((tiles,)),
        ],
        8,
        10**6,
        2 * 10**6,
        (pltpu.HBM,),
        pltpu.HBM,
    )(pltpu.with_memory_space_constraint(w_up, pltpu.HBM))
    near, far, packed = everyone(cells, packed)
    weights = lax.all_to_all(packed, "row", 0, 0, tiled=True)
    weights = weights.reshape(chan // 2, tiles * LANES)

    depth = 9 * zc
    spread = np.zeros((LANES, depth), np.float32)
    for k in range(LANES):
        for t in range(9):
            spread[k, t * zc + k % zc] = 1.0
    dims = (frames, rows, own, cols, zc, chan, chunk)
    middle = call(
        functools.partial(mid_kernel, dims),
        shape((positions, chan), bf16),
        [
            pltpu.VMEM((positions, LANES), bf16),
            pltpu.VMEM((positions, depth), bf16),
            pltpu.VMEM((frames, (rows + 2) * cols, depth), f32),
        ]
        + [pltpu.VMEM((positions, chan), bf16)] * 4
        + [pltpu.VMEM((chan, chan), bf16)] * 4
        + [pltpu.SemaphoreType.DMA((4,))],
        28,
        7 * 10**9,
        6 * 10**6,
        (pltpu.VMEM,) * 5 + (pltpu.HBM,) * 4,
    )
    added = middle(
        near,
        far,
        jnp.asarray(spread, bf16),
        w_in.reshape(3 * depth, chan),
        gain_in.reshape(1, chan),
        *(
            pltpu.with_memory_space_constraint(w, pltpu.HBM)
            for w in (w_query, w_key, w_value, w_out)
        ),
    )

    dims = (rows, cols, chan, share, chunk)
    width = 4 * LANES
    gain = gain_up.reshape(1, chan)
    fields = [
        pltpu.VMEM((rows * cols, width), f32),
        pltpu.VMEM((rows * cols, LANES), f32),
        pltpu.VMEM(((rows + 2) * cols, LANES), f32),
    ]
    fold = shape((chan, width), bf16)
    first = call(
        functools.partial(near_kernel, dims),
        (shape((count, cols, LANES), bf16), fold, fold),
        fields + [pltpu.VMEM((5 * LANES, width), bf16), pltpu.VMEM((3 * LANES, width), bf16)],
        16,
        2 * 10**9,
        3 * 10**6,
        (pltpu.VMEM,) * 3,
        (pltpu.VMEM,) * 3,
    )
    near_out, fold_all, fold_new = first(weights, added, gain)
    other = lax.ppermute(added, "row", [(k, k ^ 1) for k in range(count)])
    decoded = call(
        functools.partial(far_kernel, dims),
        shape((2 * count, cols, LANES), bf16),
        fields,
        16,
        2 * 10**9,
        3 * 10**6,
        (pltpu.VMEM,) * 5,
    )(near_out, other, fold_all, fold_new, gain)
    swapped = lax.all_to_all(decoded, ("grp", "row"), 0, 0, tiled=True)
    return call(
        functools.partial(place_kernel, share),
        shape((frames, 2 * own, 2 * cols, chan), bf16),
        [pltpu.VMEM((2 * count // 2, 2 * cols, LANES), f32)],
        8,
        10**6,
        10**6,
        (pltpu.VMEM,),
    )(swapped)


def solution(mesh):
    def body(*args):
        whole = fits(mesh, (args[0].shape, args[3].shape))
        return (whole_video if whole else per_device)(*args)

    in_specs = (
        P("grp", "row", None, None),
        P(),
        P(),
        P(),
        P(),
        P(),
        P(),
        P(),
        P(None, "row", None),
    )
    out_specs = P("grp", "row", None, None)
    return jax.shard_map(
        body, mesh=mesh, in_specs=in_specs, out_specs=out_specs, check_vma=False
    )
```

```python
import functools
import math

import jax
import jax.numpy as jnp
import numpy as np
from jax import lax
from jax.experimental import pallas as pl
from jax.experimental.pallas import tpu as pltpu
from jax.sharding import PartitionSpec as P

GROUPS = 32


norm_eps = 1e-06


def extended(cells, sides, width):
    for axis, dim in sides:
        count = lax.axis_size(axis)
        ends = count - 1
        head = lax.slice_in_dim(cells, 0, width, axis=dim)
        tail = lax.slice_in_dim(cells, cells.shape[dim] - width, cells.shape[dim], axis=dim)
        cells = jnp.concatenate(
            [
                lax.ppermute(tail, axis, [(i, (i + 1) % count) for i in range(ends)]),
                cells,
                lax.ppermute(head, axis, [((i + 1) % count, i) for i in range(ends)]),
            ],
            axis=dim,
        )
    return cells


def pad_field(rimmed):
    spaced = jnp.pad(rimmed, ((0, 0), (0, 0), (1, 1), (0, 0)))
    first_frame = spaced[:1]
    return jnp.concatenate([first_frame, first_frame, spaced], axis=0)


def tap_windows(padded, frame_count, row_count, col_count):
    windows = []
    for frame_tap in range(3):
        for row_tap in range(3):
            for col_tap in range(3):
                windows.append(
                    padded[
                        frame_tap : frame_tap + frame_count,
                        row_tap : row_tap + row_count,
                        col_tap : col_tap + col_count,
                    ]
                )
    stacked = jnp.stack(windows, axis=3)
    return stacked.reshape(frame_count * row_count * col_count, -1)


def tap_products(padded, weight, frame_count, row_count, col_count):
    running = jnp.zeros((frame_count * row_count * col_count, weight.shape[2]), jnp.float32)
    for frame_tap in range(3):
        for row_tap in range(3):
            for col_tap in range(3):
                tap_index = (frame_tap * 3 + row_tap) * 3 + col_tap
                window = padded[
                    frame_tap : frame_tap + frame_count,
                    row_tap : row_tap + row_count,
                    col_tap : col_tap + col_count,
                ]
                window = window.reshape(frame_count * row_count * col_count, -1)
                running = running + jnp.dot(
                    window, weight[tap_index], preferred_element_type=jnp.float32
                )
    return running


def group_norm(volume, gain):
    grouped = volume.astype(jnp.float32).reshape(volume.shape[:3] + (GROUPS, -1))
    entry_count = (
        volume.shape[0]
        * volume.shape[1]
        * lax.axis_size("row")
        * volume.shape[2]
        * grouped.shape[4]
    )
    group_total = lax.psum(jnp.sum(grouped, axis=(0, 1, 2, 4)), "row")
    group_avg = group_total / entry_count
    centred = grouped - group_avg[:, None]
    variance = lax.psum(jnp.sum(centred * centred, axis=(0, 1, 2, 4)), "row") / entry_count
    normal_part = centred * lax.rsqrt(variance + norm_eps)[:, None]
    return normal_part.reshape(volume.shape) * gain


def per_device(latent, w_in, gain_in, w_query, w_key, w_value, w_out, gain_up, w_up):
    frame_count, row_count, col_count, _ = latent.shape
    chan_width = w_query.shape[0]
    rimmed = extended(latent, (("row", 1),), 1)
    first_out = jnp.dot(
        tap_windows(pad_field(rimmed), frame_count, row_count, col_count),
        w_in.reshape(-1, chan_width),
        preferred_element_type=jnp.float32,
    )
    first_out = first_out.astype(jnp.bfloat16).reshape(
        frame_count, row_count, col_count, chan_width
    )
    normed = group_norm(first_out, gain_in).astype(jnp.bfloat16)
    flat_rows = normed.reshape(-1, chan_width)
    queries = jnp.dot(flat_rows, w_query, preferred_element_type=jnp.float32).astype(jnp.bfloat16)
    queries = queries.reshape(frame_count, row_count * col_count, chan_width)
    score_scale = 1.0 / math.sqrt(chan_width)
    key_table = jnp.dot(flat_rows, w_key, preferred_element_type=jnp.float32).astype(jnp.bfloat16)
    value_table = jnp.dot(flat_rows, w_value, preferred_element_type=jnp.float32).astype(
        jnp.bfloat16
    )
    key_table = key_table.reshape(frame_count, row_count, col_count, chan_width)
    value_table = value_table.reshape(frame_count, row_count, col_count, chan_width)
    row_peak = jnp.full((frame_count, row_count * col_count), -jnp.inf, jnp.float32)
    denom = jnp.zeros((frame_count, row_count * col_count), jnp.float32)
    weighted = jnp.zeros((frame_count, row_count * col_count, chan_width), jnp.float32)
    scores = (
        jnp.einsum(
            "fqd,fkd->fqk",
            queries,
            lax.all_gather(key_table, "row", axis=1, tiled=True).reshape(
                frame_count, -1, chan_width
            ),
            preferred_element_type=jnp.float32,
        )
        * score_scale
    )
    new_peak = jnp.max(scores, axis=-1)
    correction = jnp.exp(row_peak - new_peak)
    expo = jnp.exp(scores - new_peak[..., None])
    denom = denom * correction + jnp.sum(expo, axis=-1)
    weighted = weighted * correction[..., None] + jnp.einsum(
        "fqk,fkd->fqd",
        expo.astype(jnp.bfloat16),
        lax.all_gather(value_table, "row", axis=1, tiled=True).reshape(frame_count, -1, chan_width),
        preferred_element_type=jnp.float32,
    )
    row_peak, denom, weighted = (new_peak, denom, weighted)
    attended = (weighted / denom[..., None]).astype(jnp.bfloat16).reshape(-1, chan_width)
    added = first_out.astype(jnp.float32).reshape(-1, chan_width) + jnp.dot(
        attended, w_out, preferred_element_type=jnp.float32
    )
    added = added.astype(jnp.bfloat16).reshape(frame_count, row_count, col_count, chan_width)
    full_up = lax.all_gather(w_up, "row", axis=1, tiled=True)
    upsampled = jnp.repeat(jnp.repeat(added, 2, axis=1), 2, axis=2)
    up_rimmed = extended(upsampled, (("row", 1),), 1)
    padded_up = pad_field(up_rimmed)
    running = tap_products(padded_up, full_up, frame_count, 2 * row_count, 2 * col_count)
    convolved = running.astype(jnp.bfloat16).reshape(
        frame_count, 2 * row_count, 2 * col_count, chan_width
    )
    return jax.nn.silu(group_norm(convolved, gain_up)).astype(jnp.bfloat16)


LANES = 128
MIB = 1024 * 1024


def lane_iota(width):
    return lax.broadcasted_iota(jnp.int32, (1, width), 1)


def swap_blocks(arrays, width):
    arrays = list(arrays)
    block = lane_iota(LANES) // width
    step = 1
    while step < len(arrays):
        low = (block & step) == 0
        for t in range(len(arrays)):
            if t & step == 0:
                a, b = arrays[t], arrays[t | step]
                arrays[t] = jnp.where(low, a, pltpu.roll(b, step * width, 1))
                arrays[t | step] = jnp.where(low, pltpu.roll(a, LANES - step * width, 1), b)
        step *= 2
    return arrays


def group_sum(row, group):
    width = row.shape[1]
    lane = lane_iota(width)
    step = 1
    while step < group:
        low = (lane & step) == 0
        row = row + jnp.where(
            low, pltpu.roll(row, width - step, 1), pltpu.roll(row, step, 1)
        )
        step *= 2
    return row


def fold_rows(block):
    return jnp.sum(block.reshape(-1, 8, block.shape[1]), axis=0)


def all_rows(part):
    return jnp.broadcast_to(jnp.sum(part, axis=0, keepdims=True), part.shape)


def tap_tiles(taps, blocks):
    whole, rest = taps // blocks, taps % blocks
    tiles = [[(h, t * blocks + k) for k in range(blocks)] for h in range(2) for t in range(whole)]
    tail = []
    for h in range(2):
        tail += [(h, whole * blocks + k) for k in range(rest)]
        tail += [None] * (blocks // 2 - rest)
    return tiles + [tail]


def pack_kernel(w_any, out_any, w_ref, out_ref, sems, out_sems):
    taps, _, width = w_ref.shape
    groups, devices, depth, _ = out_ref.shape
    share = width // devices
    blocks = LANES // share
    first = pl.multiple_of(lax.axis_index("grp") * width, LANES)
    copies, outs = [], []
    for g in range(sems.shape[0]):
        at = slice(g * blocks, min((g + 1) * blocks, taps))
        copies.append(
            pltpu.make_async_copy(
                w_any.at[at, :, pl.ds(first, width)], w_ref.at[at], sems.at[g]
            )
        )
        copies[-1].start()
    tiles = tap_tiles(taps, blocks)
    loaded = 0
    for g in sorted(range(groups), key=lambda g: max(unit[1] for unit in tiles[g] if unit)):
        while loaded * blocks <= max(unit[1] for unit in tiles[g] if unit):
            copies[loaded].wait()
            loaded += 1
        for col in range(width // LANES):
            pieces = [
                jnp.zeros((depth, LANES), jnp.float32)
                if unit is None
                else w_ref[
                    unit[1],
                    unit[0] * depth : (unit[0] + 1) * depth,
                    col * LANES : (col + 1) * LANES,
                ].astype(jnp.float32)
                for unit in tiles[g]
            ]
            for d, piece in enumerate(swap_blocks(pieces, share)):
                out_ref[g, col * blocks + d] = piece.astype(out_ref.dtype)
        outs.append(
            pltpu.make_async_copy(
                out_ref.at[g], out_any.at[:, :, g * LANES : (g + 1) * LANES], out_sems.at[g]
            )
        )
        outs[-1].start()
    for copy in outs:
        copy.wait()


def mid_kernel(
    dims, z_ref, spread_ref, w_in_ref, gain_ref, wq_any, wk_any, wv_any, wo_any, out_ref,
    x32, wide, edge, h_ref, q_ref, k_ref, v_ref, wq_ref, wk_ref, wv_ref, wo_ref, sems,
):
    pairs = ((wq_any, wq_ref), (wk_any, wk_ref), (wv_any, wv_ref), (wo_any, wo_ref))
    loads = [pltpu.make_async_copy(a, b, sems.at[k]) for k, (a, b) in enumerate(pairs)]
    for load in loads:
        load.start()
    frames, rows, _, cols, zc, chan, chunk = dims
    per_frame = rows * cols
    total = frames * per_frame
    step = per_frame // 2
    per_tile = LANES // zc
    block = lane_iota(LANES) // zc
    first_row = lax.axis_index("row") % 2 * rows
    half = LANES // frames
    for g in range(rows // per_tile):
        tile = jnp.concatenate(
            [z_ref[first_row + g * per_tile + i] for i in range(per_tile)], 0
        ).astype(jnp.float32)
        turned = tile.T
        for f in range(frames):
            field = turned[f * half : f * half + cols]
            for i in range(per_tile):
                at = f * per_frame + (g * per_tile + i) * cols
                x32[at : at + cols, :] = jnp.where(block == i, field, 0.0).astype(x32.dtype)

    lane = lane_iota(edge.shape[2])
    col_tap = (lane // zc) % 3
    row_tap = (lane // zc) // 3
    blank = jnp.zeros((cols, edge.shape[2]), jnp.float32)
    col_index = lax.broadcasted_iota(jnp.int32, (cols, 1), 0)

    for f in range(frames):
        edge[f, 0:cols, :] = blank
        edge[f, (rows + 1) * cols : (rows + 2) * cols, :] = blank

        def columns(c, _):
            at = pl.multiple_of(f * per_frame + c * step, 16)
            v = jnp.dot(
                x32[pl.ds(at, step), :], spread_ref[...], preferred_element_type=jnp.float32
            )
            for k in range(step // cols):
                u = v[k * cols : (k + 1) * cols]
                before = jnp.where(col_index == 0, 0.0, pltpu.roll(u, 1, 0))
                after = jnp.where(col_index == cols - 1, 0.0, pltpu.roll(u, cols - 1, 0))
                u = jnp.where(col_tap == 0, before, jnp.where(col_tap == 2, after, u))
                edge[f, pl.ds(pl.multiple_of(c * step + (k + 1) * cols, 8), cols), :] = u
            return 0

        lax.fori_loop(0, per_frame // step, columns, 0)

        def lines(i, _):
            at = pl.multiple_of(i * cols, 8)
            above = edge[f, pl.ds(at, cols), :]
            here = edge[f, pl.ds(pl.multiple_of(at + cols, 8), cols), :]
            below = edge[f, pl.ds(pl.multiple_of(at + 2 * cols, 8), cols), :]
            v = jnp.where(row_tap == 0, above, jnp.where(row_tap == 2, below, here))
            wide[pl.ds(pl.multiple_of(f * per_frame + at, 16), cols), :] = v.astype(wide.dtype)
            return 0

        lax.fori_loop(0, rows, lines, 0, unroll=2)

    depth = wide.shape[1]

    def first(part):
        for f in range(frames):
            acc = None
            for dt in range(3):
                source = max(f + dt - 2, 0)
                at = source * per_frame
                term = jnp.dot(
                    wide[at : at + per_frame, :],
                    w_in_ref[dt * depth : (dt + 1) * depth, :],
                    preferred_element_type=jnp.float32,
                )
                acc = term if acc is None else acc + term
            acc = acc.astype(jnp.bfloat16)
            h_ref[slice(f * per_frame, (f + 1) * per_frame), :] = acc
            part = part + fold_rows(acc.astype(jnp.float32))
        return part

    zero = jnp.zeros((8, chan), jnp.float32)
    part = first(zero)
    group = chan // GROUPS
    count = total * group
    mean = group_sum(all_rows(part), group) / count
    mean_row = mean[0:1]

    def spreadness(c, part):
        v = h_ref[pl.ds(pl.multiple_of(c * chunk, 16), chunk), :].astype(jnp.float32) - mean_row
        return part + fold_rows(v * v)

    part = lax.fori_loop(0, total // chunk, spreadness, zero)
    variance = group_sum(all_rows(part), group) / count
    scale_row = lax.rsqrt(variance + norm_eps)[0:1]
    gain_row = gain_ref[...]

    for load in loads:
        load.wait()

    def project(c, _):
        at = pl.ds(pl.multiple_of(c * chunk, 16), chunk)
        v = h_ref[at, :].astype(jnp.float32) - mean_row
        normed = (v * scale_row * gain_row).astype(jnp.bfloat16)
        for w, o in ((wq_ref, q_ref), (wk_ref, k_ref), (wv_ref, v_ref)):
            o[at, :] = jnp.dot(normed, w[...], preferred_element_type=jnp.float32).astype(
                jnp.bfloat16
            )
        return 0

    lax.fori_loop(0, total // chunk, project, 0, unroll=total // chunk)
    score_scale = 1.0 / math.sqrt(chan)

    for f in range(frames):
        at = slice(f * per_frame, (f + 1) * per_frame)
        span = slice(f * per_frame, (f + 1) * per_frame)
        scores = lax.dot_general(
            q_ref[at, :],
            k_ref[span, :],
            (((1,), (1,)), ((), ())),
            preferred_element_type=jnp.float32,
        )
        peak = jnp.max(scores, axis=-1, keepdims=True)
        expo = jnp.exp2((scores - peak) * (score_scale * math.log2(math.e)))
        denom = jnp.sum(expo, axis=-1, keepdims=True)
        mixed = jnp.dot(
            expo.astype(jnp.bfloat16), v_ref[span, :], preferred_element_type=jnp.float32
        )
        mixed = (mixed * (1.0 / denom)).astype(jnp.bfloat16)
        shifted = jnp.dot(mixed, wo_ref[...], preferred_element_type=jnp.float32)
        out_ref[at, :] = (h_ref[at, :].astype(jnp.float32) + shifted).astype(jnp.bfloat16)


def fold_taps(w_ref, all_ref, new_ref, s_all, s_new, share):
    blocks = LANES // share
    width = s_all.shape[1]
    whole = 27 // blocks
    lane = lane_iota(width)
    inner, shift = (lane // share) % blocks, lane // LANES
    later, p, q = inner // 4 == 1, (inner // 2) % 2, inner % 2
    same = lax.broadcasted_iota(jnp.int32, (share, width), 0) == lane % share
    s_all[whole * LANES :, :] = jnp.zeros((2 * LANES, width), s_all.dtype)
    s_new[...] = jnp.zeros_like(s_new)
    for di in range(3):
        for dj in range(3):
            down = (di == 2) & (p == 1) | (di == 0) & (p == 0)
            along = (dj == 2) & (q == 1) | (dj == 0) & (q == 0)
            wanted = 2 * down.astype(jnp.int32) + along.astype(jnp.int32)
            fits_here = same & (shift == wanted)
            both, early, late = (
                jnp.where(v, 1.0, 0.0).astype(s_all.dtype)
                for v in (fits_here, fits_here & ~later, fits_here & later)
            )
            for dt in range(3):
                tap = 9 * dt + 3 * di + dj
                if tap < whole * blocks:
                    s_all[tap * share : (tap + 1) * share, :] = early if dt == 2 else both
                    if dt == 2:
                        at = (tap - (whole - 1) * blocks) * share
                        s_new[at : at + share, :] = late
                else:
                    for h in range(2):
                        at = h * (LANES + LANES // 2) + (tap - whole * blocks) * share
                        s_all[whole * LANES + at : whole * LANES + at + share, :] = early
                        s_new[LANES + at : LANES + at + share, :] = late
    tail = slice(2 * whole * LANES, (2 * whole + 1) * LANES)
    for h in range(2):
        main = slice(h * whole * LANES, (h + 1) * whole * LANES)
        last = slice(((h + 1) * whole - 1) * LANES, (h + 1) * whole * LANES)
        side = slice((whole + h) * LANES, (whole + h + 1) * LANES)
        new_side = slice((1 + h) * LANES, (2 + h) * LANES)
        for (lanes, s_ref, rows, side_rows), to_ref in (
            ((main, s_all, slice(0, whole * LANES), side), all_ref),
            ((last, s_new, slice(0, LANES), new_side), new_ref),
        ):
            v = jnp.dot(w_ref[:, lanes], s_ref[rows, :], preferred_element_type=jnp.float32)
            v += jnp.dot(w_ref[:, tail], s_ref[side_rows, :], preferred_element_type=jnp.float32)
            v = v.astype(to_ref.dtype)
            for k in range(v.shape[0] // share):
                at = (2 * k + h) * share
                to_ref[at : at + share, :] = v[k * share : (k + 1) * share]


def over_blocks(row, share):
    step = share
    while step < LANES:
        row = row + pltpu.roll(row, step, 1)
        step *= 2
    return row


def gain_kernel(share, gain_ref, out_ref):
    chan = gain_ref.shape[1]
    me = lax.axis_index("grp") * lax.axis_size("row") + lax.axis_index("row")
    gains = jnp.broadcast_to(gain_ref[...], (8, chan))
    gains = jnp.where(lane_iota(chan) // share == me, gains, 0.0)
    gains = sum(gains[:, k : k + LANES] for k in range(0, chan, LANES))
    out_ref[...] = over_blocks(gains, share)


def up_video(dims, ready, x_ref, all_ref, new_ref, gain_ref, t_ref, m0_ref, m2_ref, store):
    rows, cols, chan, share, _ = dims
    per_frame = rows * cols
    width = LANES

    ready(0)
    t_ref[...] = jnp.dot(
        x_ref[0:per_frame, :], all_ref[...], preferred_element_type=jnp.float32
    )
    ready(1)
    t_ref[...] += jnp.dot(
        x_ref[per_frame : 2 * per_frame, :], new_ref[...], preferred_element_type=jnp.float32
    )
    lane = lane_iota(width)
    right = (lane // share) % 2 == 1
    lower = (lane // (2 * share)) % 2 == 1
    col_index = lax.broadcasted_iota(jnp.int32, (cols, 1), 0)

    def beside(v):
        before = jnp.where(col_index == 0, 0.0, pltpu.roll(v, 1, 0))
        after = jnp.where(col_index == cols - 1, 0.0, pltpu.roll(v, cols - 1, 0))
        return jnp.where(right, after, before)

    blank = jnp.zeros((cols, width), jnp.float32)
    m2_ref[0:cols, :] = blank
    m2_ref[(rows + 1) * cols : (rows + 2) * cols, :] = blank

    def columns(i, _):
        at = pl.ds(pl.multiple_of(i * cols, 8), cols)
        m0_ref[at, :] = t_ref[at, 0:width] + beside(t_ref[at, width : 2 * width])
        m2_ref[pl.ds(pl.multiple_of((i + 1) * cols, 8), cols), :] = t_ref[
            at, 2 * width : 3 * width
        ] + beside(t_ref[at, 3 * width : 4 * width])
        return 0

    lax.fori_loop(0, rows, columns, 0, unroll=2)

    def lines(i, part):
        at = pl.ds(pl.multiple_of(i * cols, 8), cols)
        above = m2_ref[at, :]
        below = m2_ref[pl.ds(pl.multiple_of((i + 2) * cols, 8), cols), :]
        v = m0_ref[at, :] + jnp.where(lower, below, above)
        v = v.astype(jnp.bfloat16).astype(jnp.float32)
        m0_ref[at, :] = v
        return part + fold_rows(v)

    part = lax.fori_loop(0, rows, lines, jnp.zeros((8, width), jnp.float32), unroll=2)
    group = chan // GROUPS
    count = 2 * rows * cols * 4 * group

    def grouped(part):
        return group_sum(over_blocks(all_rows(part), share), group)

    mean_row = (grouped(part) / count)[0:1]

    def spreadness(i, part):
        v = m0_ref[pl.ds(pl.multiple_of(i * cols, 8), cols), :] - mean_row
        return part + fold_rows(v * v)

    part = lax.fori_loop(0, rows, spreadness, jnp.zeros((8, width), jnp.float32), unroll=2)
    variance = grouped(part) / count
    scale_row = (lax.rsqrt(variance + norm_eps) * gain_ref[...])[0:1]

    def finish(d, _):
        at = pl.ds(pl.multiple_of(d * cols, 8), cols)
        v = (m0_ref[at, :] - mean_row) * scale_row
        store(d, v / (1.0 + jnp.exp(-v)))
        return 0

    lax.fori_loop(0, rows, finish, 0, unroll=2)


def near_kernel(
    dims, w_ref, x_ref, gain_ref, out_ref, all_ref, new_ref, t_ref, m0_ref, m2_ref, s_all, s_new
):
    fold_taps(w_ref, all_ref, new_ref, s_all, s_new, dims[3])

    def store(d, v):
        out_ref[d] = v.astype(out_ref.dtype)

    def ready(f):
        pass

    up_video(dims, ready, x_ref, all_ref, new_ref, gain_ref, t_ref, m0_ref, m2_ref, store)


def far_kernel(
    dims, near_ref, x_any, all_ref, new_ref, gain_ref, out_ref, t_ref, m0_ref, m2_ref, x_ref, sems
):
    rows, cols = dims[:2]
    loads = []
    for f in range(2):
        at = slice(f * rows * cols, (f + 1) * rows * cols)
        loads.append(pltpu.make_async_copy(x_any.at[at], x_ref.at[at], sems.at[f]))
        loads[-1].start()
    video = lax.axis_index("row") % 2

    def keep(d, _):
        out_ref[video * rows + d] = near_ref[d]
        return 0

    lax.fori_loop(0, rows, keep, 0, unroll=4)

    def store(d, v):
        out_ref[(1 - video) * rows + d] = v.astype(out_ref.dtype)

    def ready(f):
        loads[f].wait()

    up_video(dims, ready, x_ref, all_ref, new_ref, gain_ref, t_ref, m0_ref, m2_ref, store)


def place_kernel(share, x_ref, out_ref, line):
    devices = x_ref.shape[0]
    blocks = LANES // share
    cols = x_ref.shape[1]
    for a in range(devices // blocks):
        pieces = swap_blocks(
            [x_ref[a * blocks + k].astype(jnp.float32) for k in range(blocks)], share
        )
        for half in range(blocks // 2):
            slot = a * (blocks // 2) + half
            for q in range(2):
                line[slot, pl.ds(q, cols, stride=2), :] = pieces[2 * half + q]
            out_ref[half // 2, half % 2, :, a * LANES : (a + 1) * LANES] = line[slot].astype(
                out_ref.dtype
            )


def fits(mesh, shapes):
    latent, w_query = shapes
    count = mesh.shape["row"]
    frames, own, cols, zc = latent
    chan = w_query[0]
    rows = own * count
    share = chan // (2 * count)
    return (
        mesh.shape["grp"] == 2
        and frames == 2
        and own == 1
        and count >= 8
        and count & (count - 1) == 0
        and share == 16
        and chan == 2 * count * share
        and chan == GROUPS * share
        and zc == 16
        and cols % 16 == 0
        and cols <= LANES // frames
        and (rows * cols) % 256 == 0
        and rows * cols <= 1024
    )


def call(kernel, out_shape, scratch, limit, flops, moved, spaces, out_space=pltpu.VMEM):
    return pl.pallas_call(
        kernel,
        out_shape=out_shape,
        in_specs=[pl.BlockSpec(memory_space=space) for space in spaces],
        out_specs=jax.tree.map(lambda space: pl.BlockSpec(memory_space=space), out_space),
        scratch_shapes=scratch,
        compiler_params=pltpu.CompilerParams(vmem_limit_bytes=limit * MIB),
        cost_estimate=pl.CostEstimate(flops=flops, bytes_accessed=moved, transcendentals=0),
    )


def whole_video(latent, w_in, gain_in, w_query, w_key, w_value, w_out, gain_up, w_up):
    frames, own, cols, zc = latent.shape
    chan = w_query.shape[0]
    count = lax.axis_size("row")
    rows = own * count
    positions = frames * rows * cols
    share = chan // (2 * count)
    blocks = LANES // share
    tiles = len(tap_tiles(27, blocks))
    f32, bf16 = jnp.float32, jnp.bfloat16
    shape = jax.ShapeDtypeStruct
    chunk = 256

    half = LANES // frames
    cells = jnp.swapaxes(latent.reshape(frames, cols, zc), 1, 2)
    cells = jnp.pad(cells, ((0, 0), (0, 0), (0, half - cols)))
    cells = jnp.concatenate([cells[f] for f in range(frames)], 1)
    cells = jnp.broadcast_to(cells, (2 * count, zc, LANES))
    cells = lax.all_to_all(cells, ("grp", "row"), 0, 0, tiled=True)

    pack = call(
        pack_kernel,
        shape((count, share, tiles * LANES), bf16),
        [
            pltpu.VMEM((27, 2 * share, count * share), bf16),
            pltpu.VMEM((tiles, count, share, LANES), bf16),
            pltpu.SemaphoreType.DMA((-(-27 // blocks),)),
            pltpu.SemaphoreType.DMA((tiles,)),
        ],
        8,
        10**6,
        2 * 10**6,
        (pltpu.HBM,),
        pltpu.HBM,
    )
    packed = pack(pltpu.with_memory_space_constraint(w_up, pltpu.HBM))
    weights = lax.all_to_all(packed, "row", 0, 0, tiled=True)
    weights = weights.reshape(chan // 2, tiles * LANES)

    depth = 9 * zc
    spread = np.zeros((LANES, depth), np.float32)
    for k in range(LANES):
        for t in range(9):
            spread[k, t * zc + k % zc] = 1.0
    dims = (frames, rows, own, cols, zc, chan, chunk)
    middle = call(
        functools.partial(mid_kernel, dims),
        shape((positions, chan), bf16),
        [
            pltpu.VMEM((positions, LANES), bf16),
            pltpu.VMEM((positions, depth), bf16),
            pltpu.VMEM((frames, (rows + 2) * cols, depth), f32),
        ]
        + [pltpu.VMEM((positions, chan), bf16)] * 4
        + [pltpu.VMEM((chan, chan), bf16)] * 4
        + [pltpu.SemaphoreType.DMA((4,))],
        28,
        7 * 10**9,
        6 * 10**6,
        (pltpu.VMEM,) * 4 + (pltpu.HBM,) * 4,
    )
    added = middle(
        cells,
        jnp.asarray(spread, bf16),
        w_in.reshape(3 * depth, chan),
        gain_in.reshape(1, chan),
        *(
            pltpu.with_memory_space_constraint(w, pltpu.HBM)
            for w in (w_query, w_key, w_value, w_out)
        ),
    )

    dims = (rows, cols, chan, share, chunk)
    width = 4 * LANES
    gains = call(
        functools.partial(gain_kernel, share), shape((8, LANES), f32), [], 1, 10**4, 10**4,
        (pltpu.VMEM,),
    )
    gain = gains(gain_up.reshape(1, chan))
    fields = [
        pltpu.VMEM((rows * cols, width), f32),
        pltpu.VMEM((rows * cols, LANES), f32),
        pltpu.VMEM(((rows + 2) * cols, LANES), f32),
    ]
    fold = shape((chan, width), bf16)
    first = call(
        functools.partial(near_kernel, dims),
        (shape((count, cols, LANES), bf16), fold, fold),
        fields + [pltpu.VMEM((5 * LANES, width), bf16), pltpu.VMEM((3 * LANES, width), bf16)],
        16,
        2 * 10**9,
        3 * 10**6,
        (pltpu.VMEM,) * 3,
        (pltpu.VMEM,) * 3,
    )
    near_out, fold_all, fold_new = first(weights, added, gain)
    other = lax.ppermute(added, "row", [(k, k ^ 1) for k in range(count)])
    decoded = call(
        functools.partial(far_kernel, dims),
        shape((2 * count, cols, LANES), bf16),
        fields + [pltpu.VMEM(added.shape, bf16), pltpu.SemaphoreType.DMA((2,))],
        16,
        2 * 10**9,
        3 * 10**6,
        (pltpu.VMEM, pltpu.HBM) + (pltpu.VMEM,) * 3,
    )(near_out, pltpu.with_memory_space_constraint(other, pltpu.HBM), fold_all, fold_new, gain)
    swapped = lax.all_to_all(decoded, ("grp", "row"), 0, 0, tiled=True)
    return call(
        functools.partial(place_kernel, share),
        shape((frames, 2 * own, 2 * cols, chan), bf16),
        [pltpu.VMEM((2 * count // 2, 2 * cols, LANES), f32)],
        8,
        10**6,
        10**6,
        (pltpu.VMEM,),
    )(swapped)


def solution(mesh):
    def body(*args):
        whole = fits(mesh, (args[0].shape, args[3].shape))
        return (whole_video if whole else per_device)(*args)

    in_specs = (
        P("grp", "row", None, None),
        P(),
        P(),
        P(),
        P(),
        P(),
        P(),
        P(),
        P(None, "row", None),
    )
    out_specs = P("grp", "row", None, None)
    return jax.shard_map(
        body, mesh=mesh, in_specs=in_specs, out_specs=out_specs, check_vma=False
    )
```

```python
import functools
import math

import jax
import jax.numpy as jnp
import numpy as np
from jax import lax
from jax.experimental import pallas as pl
from jax.experimental.pallas import tpu as pltpu
from jax.sharding import PartitionSpec as P

GROUPS = 32


norm_eps = 1e-06


def extended(cells, sides, width):
    for axis, dim in sides:
        count = lax.axis_size(axis)
        ends = count - 1
        head = lax.slice_in_dim(cells, 0, width, axis=dim)
        tail = lax.slice_in_dim(cells, cells.shape[dim] - width, cells.shape[dim], axis=dim)
        cells = jnp.concatenate(
            [
                lax.ppermute(tail, axis, [(i, (i + 1) % count) for i in range(ends)]),
                cells,
                lax.ppermute(head, axis, [((i + 1) % count, i) for i in range(ends)]),
            ],
            axis=dim,
        )
    return cells


def pad_field(rimmed):
    spaced = jnp.pad(rimmed, ((0, 0), (0, 0), (1, 1), (0, 0)))
    first_frame = spaced[:1]
    return jnp.concatenate([first_frame, first_frame, spaced], axis=0)


def tap_windows(padded, frame_count, row_count, col_count):
    windows = []
    for frame_tap in range(3):
        for row_tap in range(3):
            for col_tap in range(3):
                windows.append(
                    padded[
                        frame_tap : frame_tap + frame_count,
                        row_tap : row_tap + row_count,
                        col_tap : col_tap + col_count,
                    ]
                )
    stacked = jnp.stack(windows, axis=3)
    return stacked.reshape(frame_count * row_count * col_count, -1)


def tap_products(padded, weight, frame_count, row_count, col_count):
    running = jnp.zeros((frame_count * row_count * col_count, weight.shape[2]), jnp.float32)
    for frame_tap in range(3):
        for row_tap in range(3):
            for col_tap in range(3):
                tap_index = (frame_tap * 3 + row_tap) * 3 + col_tap
                window = padded[
                    frame_tap : frame_tap + frame_count,
                    row_tap : row_tap + row_count,
                    col_tap : col_tap + col_count,
                ]
                window = window.reshape(frame_count * row_count * col_count, -1)
                running = running + jnp.dot(
                    window, weight[tap_index], preferred_element_type=jnp.float32
                )
    return running


def group_norm(volume, gain):
    grouped = volume.astype(jnp.float32).reshape(volume.shape[:3] + (GROUPS, -1))
    entry_count = (
        volume.shape[0]
        * volume.shape[1]
        * lax.axis_size("row")
        * volume.shape[2]
        * grouped.shape[4]
    )
    group_total = lax.psum(jnp.sum(grouped, axis=(0, 1, 2, 4)), "row")
    group_avg = group_total / entry_count
    centred = grouped - group_avg[:, None]
    variance = lax.psum(jnp.sum(centred * centred, axis=(0, 1, 2, 4)), "row") / entry_count
    normal_part = centred * lax.rsqrt(variance + norm_eps)[:, None]
    return normal_part.reshape(volume.shape) * gain


def per_device(latent, w_in, gain_in, w_query, w_key, w_value, w_out, gain_up, w_up):
    frame_count, row_count, col_count, _ = latent.shape
    chan_width = w_query.shape[0]
    rimmed = extended(latent, (("row", 1),), 1)
    first_out = jnp.dot(
        tap_windows(pad_field(rimmed), frame_count, row_count, col_count),
        w_in.reshape(-1, chan_width),
        preferred_element_type=jnp.float32,
    )
    first_out = first_out.astype(jnp.bfloat16).reshape(
        frame_count, row_count, col_count, chan_width
    )
    normed = group_norm(first_out, gain_in).astype(jnp.bfloat16)
    flat_rows = normed.reshape(-1, chan_width)
    queries = jnp.dot(flat_rows, w_query, preferred_element_type=jnp.float32).astype(jnp.bfloat16)
    queries = queries.reshape(frame_count, row_count * col_count, chan_width)
    score_scale = 1.0 / math.sqrt(chan_width)
    key_table = jnp.dot(flat_rows, w_key, preferred_element_type=jnp.float32).astype(jnp.bfloat16)
    value_table = jnp.dot(flat_rows, w_value, preferred_element_type=jnp.float32).astype(
        jnp.bfloat16
    )
    key_table = key_table.reshape(frame_count, row_count, col_count, chan_width)
    value_table = value_table.reshape(frame_count, row_count, col_count, chan_width)
    row_peak = jnp.full((frame_count, row_count * col_count), -jnp.inf, jnp.float32)
    denom = jnp.zeros((frame_count, row_count * col_count), jnp.float32)
    weighted = jnp.zeros((frame_count, row_count * col_count, chan_width), jnp.float32)
    scores = (
        jnp.einsum(
            "fqd,fkd->fqk",
            queries,
            lax.all_gather(key_table, "row", axis=1, tiled=True).reshape(
                frame_count, -1, chan_width
            ),
            preferred_element_type=jnp.float32,
        )
        * score_scale
    )
    new_peak = jnp.max(scores, axis=-1)
    correction = jnp.exp(row_peak - new_peak)
    expo = jnp.exp(scores - new_peak[..., None])
    denom = denom * correction + jnp.sum(expo, axis=-1)
    weighted = weighted * correction[..., None] + jnp.einsum(
        "fqk,fkd->fqd",
        expo.astype(jnp.bfloat16),
        lax.all_gather(value_table, "row", axis=1, tiled=True).reshape(frame_count, -1, chan_width),
        preferred_element_type=jnp.float32,
    )
    row_peak, denom, weighted = (new_peak, denom, weighted)
    attended = (weighted / denom[..., None]).astype(jnp.bfloat16).reshape(-1, chan_width)
    added = first_out.astype(jnp.float32).reshape(-1, chan_width) + jnp.dot(
        attended, w_out, preferred_element_type=jnp.float32
    )
    added = added.astype(jnp.bfloat16).reshape(frame_count, row_count, col_count, chan_width)
    full_up = lax.all_gather(w_up, "row", axis=1, tiled=True)
    upsampled = jnp.repeat(jnp.repeat(added, 2, axis=1), 2, axis=2)
    up_rimmed = extended(upsampled, (("row", 1),), 1)
    padded_up = pad_field(up_rimmed)
    running = tap_products(padded_up, full_up, frame_count, 2 * row_count, 2 * col_count)
    convolved = running.astype(jnp.bfloat16).reshape(
        frame_count, 2 * row_count, 2 * col_count, chan_width
    )
    return jax.nn.silu(group_norm(convolved, gain_up)).astype(jnp.bfloat16)


LANES = 128
MIB = 1024 * 1024


def lane_iota(width):
    return lax.broadcasted_iota(jnp.int32, (1, width), 1)


def swap_blocks(arrays, width):
    arrays = list(arrays)
    block = lane_iota(LANES) // width
    step = 1
    while step < len(arrays):
        low = (block & step) == 0
        for t in range(len(arrays)):
            if t & step == 0:
                a, b = arrays[t], arrays[t | step]
                arrays[t] = jnp.where(low, a, pltpu.roll(b, step * width, 1))
                arrays[t | step] = jnp.where(low, pltpu.roll(a, LANES - step * width, 1), b)
        step *= 2
    return arrays


def group_sum(row, group):
    width = row.shape[1]
    lane = lane_iota(width)
    step = 1
    while step < group:
        low = (lane & step) == 0
        row = row + jnp.where(
            low, pltpu.roll(row, width - step, 1), pltpu.roll(row, step, 1)
        )
        step *= 2
    return row


def fold_rows(block):
    return jnp.sum(block.reshape(-1, 8, block.shape[1]), axis=0)


def all_rows(part):
    return jnp.broadcast_to(jnp.sum(part, axis=0, keepdims=True), part.shape)


def tap_tiles(taps, blocks):
    whole, rest = taps // blocks, taps % blocks
    tiles = [[(h, t * blocks + k) for k in range(blocks)] for h in range(2) for t in range(whole)]
    tail = []
    for h in range(2):
        tail += [(h, whole * blocks + k) for k in range(rest)]
        tail += [None] * (blocks // 2 - rest)
    return tiles + [tail]


def pack_kernel(w_any, out_any, w_ref, out_ref, sems, out_sems):
    taps, _, width = w_ref.shape
    groups, devices, depth, _ = out_ref.shape
    share = width // devices
    blocks = LANES // share
    first = pl.multiple_of(lax.axis_index("grp") * width, LANES)
    copies, outs = [], []
    for g in range(sems.shape[0]):
        at = slice(g * blocks, min((g + 1) * blocks, taps))
        copies.append(
            pltpu.make_async_copy(
                w_any.at[at, :, pl.ds(first, width)], w_ref.at[at], sems.at[g]
            )
        )
        copies[-1].start()
    tiles = tap_tiles(taps, blocks)
    loaded = 0
    for g in sorted(range(groups), key=lambda g: max(unit[1] for unit in tiles[g] if unit)):
        while loaded * blocks <= max(unit[1] for unit in tiles[g] if unit):
            copies[loaded].wait()
            loaded += 1
        for col in range(width // LANES):
            pieces = [
                jnp.zeros((depth, LANES), jnp.float32)
                if unit is None
                else w_ref[
                    unit[1],
                    unit[0] * depth : (unit[0] + 1) * depth,
                    col * LANES : (col + 1) * LANES,
                ].astype(jnp.float32)
                for unit in tiles[g]
            ]
            for d, piece in enumerate(swap_blocks(pieces, share)):
                out_ref[g, col * blocks + d] = piece.astype(out_ref.dtype)
        outs.append(
            pltpu.make_async_copy(
                out_ref.at[g], out_any.at[:, :, g * LANES : (g + 1) * LANES], out_sems.at[g]
            )
        )
        outs[-1].start()
    for copy in outs:
        copy.wait()


def mid_kernel(
    dims, z_ref, spread_ref, w_in_ref, gain_ref, wq_any, wk_any, wv_any, wo_any, out_ref,
    x32, wide, edge, h_ref, q_ref, k_ref, v_ref, wq_ref, wk_ref, wv_ref, wo_ref, sems,
):
    pairs = ((wq_any, wq_ref), (wk_any, wk_ref), (wv_any, wv_ref), (wo_any, wo_ref))
    loads = [pltpu.make_async_copy(a, b, sems.at[k]) for k, (a, b) in enumerate(pairs)]
    for load in loads:
        load.start()
    frames, rows, _, cols, zc, chan, chunk = dims
    per_frame = rows * cols
    total = frames * per_frame
    step = per_frame // 2
    per_tile = LANES // zc
    block = lane_iota(LANES) // zc
    first_row = lax.axis_index("row") % 2 * rows
    half = LANES // frames
    for g in range(rows // per_tile):
        tile = jnp.concatenate(
            [z_ref[first_row + g * per_tile + i] for i in range(per_tile)], 0
        ).astype(jnp.float32)
        turned = tile.T
        for f in range(frames):
            field = turned[f * half : f * half + cols]
            for i in range(per_tile):
                at = f * per_frame + (g * per_tile + i) * cols
                x32[at : at + cols, :] = jnp.where(block == i, field, 0.0).astype(x32.dtype)

    lane = lane_iota(edge.shape[2])
    col_tap = (lane // zc) % 3
    row_tap = (lane // zc) // 3
    blank = jnp.zeros((cols, edge.shape[2]), jnp.float32)
    col_index = lax.broadcasted_iota(jnp.int32, (cols, 1), 0)

    for f in range(frames):
        edge[f, 0:cols, :] = blank
        edge[f, (rows + 1) * cols : (rows + 2) * cols, :] = blank

        def columns(c, _):
            at = pl.multiple_of(f * per_frame + c * step, 16)
            v = jnp.dot(
                x32[pl.ds(at, step), :], spread_ref[...], preferred_element_type=jnp.float32
            )
            for k in range(step // cols):
                u = v[k * cols : (k + 1) * cols]
                before = jnp.where(col_index == 0, 0.0, pltpu.roll(u, 1, 0))
                after = jnp.where(col_index == cols - 1, 0.0, pltpu.roll(u, cols - 1, 0))
                u = jnp.where(col_tap == 0, before, jnp.where(col_tap == 2, after, u))
                edge[f, pl.ds(pl.multiple_of(c * step + (k + 1) * cols, 8), cols), :] = u
            return 0

        lax.fori_loop(0, per_frame // step, columns, 0)

        def lines(i, _):
            at = pl.multiple_of(i * cols, 8)
            above = edge[f, pl.ds(at, cols), :]
            here = edge[f, pl.ds(pl.multiple_of(at + cols, 8), cols), :]
            below = edge[f, pl.ds(pl.multiple_of(at + 2 * cols, 8), cols), :]
            v = jnp.where(row_tap == 0, above, jnp.where(row_tap == 2, below, here))
            wide[pl.ds(pl.multiple_of(f * per_frame + at, 16), cols), :] = v.astype(wide.dtype)
            return 0

        lax.fori_loop(0, rows, lines, 0, unroll=2)

    depth = wide.shape[1]

    def first(part):
        for f in range(frames):
            acc = None
            for dt in range(3):
                source = max(f + dt - 2, 0)
                at = source * per_frame
                term = jnp.dot(
                    wide[at : at + per_frame, :],
                    w_in_ref[dt * depth : (dt + 1) * depth, :],
                    preferred_element_type=jnp.float32,
                )
                acc = term if acc is None else acc + term
            acc = acc.astype(jnp.bfloat16)
            h_ref[slice(f * per_frame, (f + 1) * per_frame), :] = acc
            part = part + fold_rows(acc.astype(jnp.float32))
        return part

    zero = jnp.zeros((8, chan), jnp.float32)
    part = first(zero)
    group = chan // GROUPS
    count = total * group
    mean = group_sum(all_rows(part), group) / count
    mean_row = mean[0:1]

    def spreadness(c, part):
        v = h_ref[pl.ds(pl.multiple_of(c * chunk, 16), chunk), :].astype(jnp.float32) - mean_row
        return part + fold_rows(v * v)

    part = lax.fori_loop(0, total // chunk, spreadness, zero)
    variance = group_sum(all_rows(part), group) / count
    scale_row = lax.rsqrt(variance + norm_eps)[0:1]
    gain_row = gain_ref[...]

    for load in loads:
        load.wait()

    def project(c, _):
        at = pl.ds(pl.multiple_of(c * chunk, 16), chunk)
        v = h_ref[at, :].astype(jnp.float32) - mean_row
        normed = (v * scale_row * gain_row).astype(jnp.bfloat16)
        for w, o in ((wq_ref, q_ref), (wk_ref, k_ref), (wv_ref, v_ref)):
            o[at, :] = jnp.dot(normed, w[...], preferred_element_type=jnp.float32).astype(
                jnp.bfloat16
            )
        return 0

    lax.fori_loop(0, total // chunk, project, 0, unroll=total // chunk)
    score_scale = 1.0 / math.sqrt(chan)

    for f in range(frames):
        at = slice(f * per_frame, (f + 1) * per_frame)
        span = slice(f * per_frame, (f + 1) * per_frame)
        scores = lax.dot_general(
            q_ref[at, :],
            k_ref[span, :],
            (((1,), (1,)), ((), ())),
            preferred_element_type=jnp.float32,
        )
        peak = jnp.max(scores, axis=-1, keepdims=True)
        expo = jnp.exp2((scores - peak) * (score_scale * math.log2(math.e)))
        denom = jnp.sum(expo, axis=-1, keepdims=True)
        mixed = jnp.dot(
            expo.astype(jnp.bfloat16), v_ref[span, :], preferred_element_type=jnp.float32
        )
        mixed = (mixed * (1.0 / denom)).astype(jnp.bfloat16)
        shifted = jnp.dot(mixed, wo_ref[...], preferred_element_type=jnp.float32)
        out_ref[at, :] = (h_ref[at, :].astype(jnp.float32) + shifted).astype(jnp.bfloat16)


def fold_taps(w_ref, all_ref, new_ref, s_all, s_new, share):
    blocks = LANES // share
    width = s_all.shape[1]
    whole = 27 // blocks
    lane = lane_iota(width)
    inner, shift = (lane // share) % blocks, lane // LANES
    later, p, q = inner // 4 == 1, (inner // 2) % 2, inner % 2
    same = lax.broadcasted_iota(jnp.int32, (share, width), 0) == lane % share
    s_all[whole * LANES :, :] = jnp.zeros((2 * LANES, width), s_all.dtype)
    s_new[...] = jnp.zeros_like(s_new)
    for di in range(3):
        for dj in range(3):
            down = (di == 2) & (p == 1) | (di == 0) & (p == 0)
            along = (dj == 2) & (q == 1) | (dj == 0) & (q == 0)
            wanted = 2 * down.astype(jnp.int32) + along.astype(jnp.int32)
            fits_here = same & (shift == wanted)
            both, early, late = (
                jnp.where(v, 1.0, 0.0).astype(s_all.dtype)
                for v in (fits_here, fits_here & ~later, fits_here & later)
            )
            for dt in range(3):
                tap = 9 * dt + 3 * di + dj
                if tap < whole * blocks:
                    s_all[tap * share : (tap + 1) * share, :] = early if dt == 2 else both
                    if dt == 2:
                        at = (tap - (whole - 1) * blocks) * share
                        s_new[at : at + share, :] = late
                else:
                    for h in range(2):
                        at = h * (LANES + LANES // 2) + (tap - whole * blocks) * share
                        s_all[whole * LANES + at : whole * LANES + at + share, :] = early
                        s_new[LANES + at : LANES + at + share, :] = late
    tail = slice(2 * whole * LANES, (2 * whole + 1) * LANES)
    for h in range(2):
        main = slice(h * whole * LANES, (h + 1) * whole * LANES)
        last = slice(((h + 1) * whole - 1) * LANES, (h + 1) * whole * LANES)
        side = slice((whole + h) * LANES, (whole + h + 1) * LANES)
        new_side = slice((1 + h) * LANES, (2 + h) * LANES)
        for (lanes, s_ref, rows, side_rows), to_ref in (
            ((main, s_all, slice(0, whole * LANES), side), all_ref),
            ((last, s_new, slice(0, LANES), new_side), new_ref),
        ):
            v = jnp.dot(w_ref[:, lanes], s_ref[rows, :], preferred_element_type=jnp.float32)
            v += jnp.dot(w_ref[:, tail], s_ref[side_rows, :], preferred_element_type=jnp.float32)
            v = v.astype(to_ref.dtype)
            for k in range(v.shape[0] // share):
                at = (2 * k + h) * share
                to_ref[at : at + share, :] = v[k * share : (k + 1) * share]


def over_blocks(row, share):
    step = share
    while step < LANES:
        row = row + pltpu.roll(row, step, 1)
        step *= 2
    return row


def gain_kernel(share, gain_ref, out_ref):
    chan = gain_ref.shape[1]
    me = lax.axis_index("grp") * lax.axis_size("row") + lax.axis_index("row")
    gains = jnp.broadcast_to(gain_ref[...], (8, chan))
    gains = jnp.where(lane_iota(chan) // share == me, gains, 0.0)
    gains = sum(gains[:, k : k + LANES] for k in range(0, chan, LANES))
    out_ref[...] = over_blocks(gains, share)


def up_video(dims, ready, x_ref, all_ref, new_ref, gain_ref, t_ref, m0_ref, m2_ref, store):
    rows, cols, chan, share, _ = dims
    per_frame = rows * cols
    width = LANES

    ready(0)
    t_ref[...] = jnp.dot(
        x_ref[0:per_frame, :], all_ref[...], preferred_element_type=jnp.float32
    )
    ready(1)
    t_ref[...] += jnp.dot(
        x_ref[per_frame : 2 * per_frame, :], new_ref[...], preferred_element_type=jnp.float32
    )
    lane = lane_iota(width)
    right = (lane // share) % 2 == 1
    lower = (lane // (2 * share)) % 2 == 1
    col_index = lax.broadcasted_iota(jnp.int32, (cols, 1), 0)

    def beside(v):
        before = jnp.where(col_index == 0, 0.0, pltpu.roll(v, 1, 0))
        after = jnp.where(col_index == cols - 1, 0.0, pltpu.roll(v, cols - 1, 0))
        return jnp.where(right, after, before)

    blank = jnp.zeros((cols, width), jnp.float32)
    m2_ref[0:cols, :] = blank
    m2_ref[(rows + 1) * cols : (rows + 2) * cols, :] = blank

    def columns(i, _):
        at = pl.ds(pl.multiple_of(i * cols, 8), cols)
        m0_ref[at, :] = t_ref[at, 0:width] + beside(t_ref[at, width : 2 * width])
        m2_ref[pl.ds(pl.multiple_of((i + 1) * cols, 8), cols), :] = t_ref[
            at, 2 * width : 3 * width
        ] + beside(t_ref[at, 3 * width : 4 * width])
        return 0

    lax.fori_loop(0, rows, columns, 0, unroll=rows)

    def lines(i, part):
        at = pl.ds(pl.multiple_of(i * cols, 8), cols)
        above = m2_ref[at, :]
        below = m2_ref[pl.ds(pl.multiple_of((i + 2) * cols, 8), cols), :]
        v = m0_ref[at, :] + jnp.where(lower, below, above)
        v = v.astype(jnp.bfloat16).astype(jnp.float32)
        m0_ref[at, :] = v
        return part + fold_rows(v)

    part = lax.fori_loop(0, rows, lines, jnp.zeros((8, width), jnp.float32), unroll=rows)
    group = chan // GROUPS
    count = 2 * rows * cols * 4 * group

    def grouped(part):
        return group_sum(over_blocks(all_rows(part), share), group)

    mean_row = (grouped(part) / count)[0:1]

    def spreadness(i, part):
        v = m0_ref[pl.ds(pl.multiple_of(i * cols, 8), cols), :] - mean_row
        return part + fold_rows(v * v)

    part = lax.fori_loop(0, rows, spreadness, jnp.zeros((8, width), jnp.float32), unroll=rows)
    variance = grouped(part) / count
    scale_row = (lax.rsqrt(variance + norm_eps) * gain_ref[...])[0:1]

    def finish(d, _):
        at = pl.ds(pl.multiple_of(d * cols, 8), cols)
        v = (m0_ref[at, :] - mean_row) * scale_row
        store(d, v / (1.0 + jnp.exp(-v)))
        return 0

    lax.fori_loop(0, rows, finish, 0, unroll=rows)


def near_kernel(
    dims, w_ref, x_ref, gain_ref, out_ref, all_ref, new_ref, t_ref, m0_ref, m2_ref, s_all, s_new
):
    fold_taps(w_ref, all_ref, new_ref, s_all, s_new, dims[3])

    def store(d, v):
        out_ref[d] = v.astype(out_ref.dtype)

    def ready(f):
        pass

    up_video(dims, ready, x_ref, all_ref, new_ref, gain_ref, t_ref, m0_ref, m2_ref, store)


def far_kernel(
    dims, near_ref, x_any, all_ref, new_ref, gain_ref, out_ref, t_ref, m0_ref, m2_ref, x_ref, sems
):
    rows, cols = dims[:2]
    loads = []
    for f in range(2):
        at = slice(f * rows * cols, (f + 1) * rows * cols)
        loads.append(pltpu.make_async_copy(x_any.at[at], x_ref.at[at], sems.at[f]))
        loads[-1].start()
    video = lax.axis_index("row") % 2

    def keep(d, _):
        out_ref[video * rows + d] = near_ref[d]
        return 0

    lax.fori_loop(0, rows, keep, 0, unroll=4)

    def store(d, v):
        out_ref[(1 - video) * rows + d] = v.astype(out_ref.dtype)

    def ready(f):
        loads[f].wait()

    up_video(dims, ready, x_ref, all_ref, new_ref, gain_ref, t_ref, m0_ref, m2_ref, store)


def place_kernel(share, x_ref, out_ref, line):
    devices = x_ref.shape[0]
    blocks = LANES // share
    cols = x_ref.shape[1]
    for a in range(devices // blocks):
        pieces = swap_blocks(
            [x_ref[a * blocks + k].astype(jnp.float32) for k in range(blocks)], share
        )
        for half in range(blocks // 2):
            slot = a * (blocks // 2) + half
            for q in range(2):
                line[slot, pl.ds(q, cols, stride=2), :] = pieces[2 * half + q]
            out_ref[half // 2, half % 2, :, a * LANES : (a + 1) * LANES] = line[slot].astype(
                out_ref.dtype
            )


def fits(mesh, shapes):
    latent, w_query = shapes
    count = mesh.shape["row"]
    frames, own, cols, zc = latent
    chan = w_query[0]
    rows = own * count
    share = chan // (2 * count)
    return (
        mesh.shape["grp"] == 2
        and frames == 2
        and own == 1
        and count >= 8
        and count & (count - 1) == 0
        and share == 16
        and chan == 2 * count * share
        and chan == GROUPS * share
        and zc == 16
        and cols % 16 == 0
        and cols <= LANES // frames
        and (rows * cols) % 256 == 0
        and rows * cols <= 1024
    )


def call(kernel, out_shape, scratch, limit, flops, moved, spaces, out_space=pltpu.VMEM):
    return pl.pallas_call(
        kernel,
        out_shape=out_shape,
        in_specs=[pl.BlockSpec(memory_space=space) for space in spaces],
        out_specs=jax.tree.map(lambda space: pl.BlockSpec(memory_space=space), out_space),
        scratch_shapes=scratch,
        compiler_params=pltpu.CompilerParams(vmem_limit_bytes=limit * MIB),
        cost_estimate=pl.CostEstimate(flops=flops, bytes_accessed=moved, transcendentals=0),
    )


def whole_video(latent, w_in, gain_in, w_query, w_key, w_value, w_out, gain_up, w_up):
    frames, own, cols, zc = latent.shape
    chan = w_query.shape[0]
    count = lax.axis_size("row")
    rows = own * count
    positions = frames * rows * cols
    share = chan // (2 * count)
    blocks = LANES // share
    tiles = len(tap_tiles(27, blocks))
    f32, bf16 = jnp.float32, jnp.bfloat16
    shape = jax.ShapeDtypeStruct
    chunk = 256

    half = LANES // frames
    cells = jnp.swapaxes(latent.reshape(frames, cols, zc), 1, 2)
    cells = jnp.pad(cells, ((0, 0), (0, 0), (0, half - cols)))
    cells = jnp.concatenate([cells[f] for f in range(frames)], 1)
    cells = jnp.broadcast_to(cells, (2 * count, zc, LANES))
    cells = lax.all_to_all(cells, ("grp", "row"), 0, 0, tiled=True)

    pack = call(
        pack_kernel,
        shape((count, share, tiles * LANES), bf16),
        [
            pltpu.VMEM((27, 2 * share, count * share), bf16),
            pltpu.VMEM((tiles, count, share, LANES), bf16),
            pltpu.SemaphoreType.DMA((-(-27 // blocks),)),
            pltpu.SemaphoreType.DMA((tiles,)),
        ],
        8,
        10**6,
        2 * 10**6,
        (pltpu.HBM,),
        pltpu.HBM,
    )
    packed = pack(pltpu.with_memory_space_constraint(w_up, pltpu.HBM))
    weights = lax.all_to_all(packed, "row", 0, 0, tiled=True)
    weights = weights.reshape(chan // 2, tiles * LANES)

    depth = 9 * zc
    spread = np.zeros((LANES, depth), np.float32)
    for k in range(LANES):
        for t in range(9):
            spread[k, t * zc + k % zc] = 1.0
    dims = (frames, rows, own, cols, zc, chan, chunk)
    middle = call(
        functools.partial(mid_kernel, dims),
        shape((positions, chan), bf16),
        [
            pltpu.VMEM((positions, LANES), bf16),
            pltpu.VMEM((positions, depth), bf16),
            pltpu.VMEM((frames, (rows + 2) * cols, depth), f32),
        ]
        + [pltpu.VMEM((positions, chan), bf16)] * 4
        + [pltpu.VMEM((chan, chan), bf16)] * 4
        + [pltpu.SemaphoreType.DMA((4,))],
        28,
        7 * 10**9,
        6 * 10**6,
        (pltpu.VMEM,) * 4 + (pltpu.HBM,) * 4,
    )
    added = middle(
        cells,
        jnp.asarray(spread, bf16),
        w_in.reshape(3 * depth, chan),
        gain_in.reshape(1, chan),
        *(
            pltpu.with_memory_space_constraint(w, pltpu.HBM)
            for w in (w_query, w_key, w_value, w_out)
        ),
    )

    dims = (rows, cols, chan, share, chunk)
    width = 4 * LANES
    gains = call(
        functools.partial(gain_kernel, share), shape((8, LANES), f32), [], 1, 10**4, 10**4,
        (pltpu.VMEM,),
    )
    gain = gains(gain_up.reshape(1, chan))
    fields = [
        pltpu.VMEM((rows * cols, width), f32),
        pltpu.VMEM((rows * cols, LANES), f32),
        pltpu.VMEM(((rows + 2) * cols, LANES), f32),
    ]
    fold = shape((chan, width), bf16)
    first = call(
        functools.partial(near_kernel, dims),
        (shape((count, cols, LANES), bf16), fold, fold),
        fields + [pltpu.VMEM((5 * LANES, width), bf16), pltpu.VMEM((3 * LANES, width), bf16)],
        16,
        2 * 10**9,
        3 * 10**6,
        (pltpu.VMEM,) * 3,
        (pltpu.VMEM,) * 3,
    )
    near_out, fold_all, fold_new = first(weights, added, gain)
    other = lax.ppermute(added, "row", [(k, k ^ 1) for k in range(count)])
    decoded = call(
        functools.partial(far_kernel, dims),
        shape((2 * count, cols, LANES), bf16),
        fields + [pltpu.VMEM(added.shape, bf16), pltpu.SemaphoreType.DMA((2,))],
        16,
        2 * 10**9,
        3 * 10**6,
        (pltpu.VMEM, pltpu.HBM) + (pltpu.VMEM,) * 3,
    )(near_out, pltpu.with_memory_space_constraint(other, pltpu.HBM), fold_all, fold_new, gain)
    swapped = lax.all_to_all(decoded, ("grp", "row"), 0, 0, tiled=True)
    return call(
        functools.partial(place_kernel, share),
        shape((frames, 2 * own, 2 * cols, chan), bf16),
        [pltpu.VMEM((2 * count // 2, 2 * cols, LANES), f32)],
        8,
        10**6,
        10**6,
        (pltpu.VMEM,),
    )(swapped)


def solution(mesh):
    def body(*args):
        whole = fits(mesh, (args[0].shape, args[3].shape))
        return (whole_video if whole else per_device)(*args)

    in_specs = (
        P("grp", "row", None, None),
        P(),
        P(),
        P(),
        P(),
        P(),
        P(),
        P(),
        P(None, "row", None),
    )
    out_specs = P("grp", "row", None, None)
    return jax.shard_map(
        body, mesh=mesh, in_specs=in_specs, out_specs=out_specs, check_vma=False
    )
```

```python
import functools
import math

import jax
import jax.numpy as jnp
import numpy as np
from jax import lax
from jax.experimental import pallas as pl
from jax.experimental.pallas import tpu as pltpu
from jax.sharding import PartitionSpec as P

GROUPS = 32


norm_eps = 1e-06


def extended(cells, sides, width):
    for axis, dim in sides:
        count = lax.axis_size(axis)
        ends = count - 1
        head = lax.slice_in_dim(cells, 0, width, axis=dim)
        tail = lax.slice_in_dim(cells, cells.shape[dim] - width, cells.shape[dim], axis=dim)
        cells = jnp.concatenate(
            [
                lax.ppermute(tail, axis, [(i, (i + 1) % count) for i in range(ends)]),
                cells,
                lax.ppermute(head, axis, [((i + 1) % count, i) for i in range(ends)]),
            ],
            axis=dim,
        )
    return cells


def pad_field(rimmed):
    spaced = jnp.pad(rimmed, ((0, 0), (0, 0), (1, 1), (0, 0)))
    first_frame = spaced[:1]
    return jnp.concatenate([first_frame, first_frame, spaced], axis=0)


def tap_windows(padded, frame_count, row_count, col_count):
    windows = []
    for frame_tap in range(3):
        for row_tap in range(3):
            for col_tap in range(3):
                windows.append(
                    padded[
                        frame_tap : frame_tap + frame_count,
                        row_tap : row_tap + row_count,
                        col_tap : col_tap + col_count,
                    ]
                )
    stacked = jnp.stack(windows, axis=3)
    return stacked.reshape(frame_count * row_count * col_count, -1)


def tap_products(padded, weight, frame_count, row_count, col_count):
    running = jnp.zeros((frame_count * row_count * col_count, weight.shape[2]), jnp.float32)
    for frame_tap in range(3):
        for row_tap in range(3):
            for col_tap in range(3):
                tap_index = (frame_tap * 3 + row_tap) * 3 + col_tap
                window = padded[
                    frame_tap : frame_tap + frame_count,
                    row_tap : row_tap + row_count,
                    col_tap : col_tap + col_count,
                ]
                window = window.reshape(frame_count * row_count * col_count, -1)
                running = running + jnp.dot(
                    window, weight[tap_index], preferred_element_type=jnp.float32
                )
    return running


def group_norm(volume, gain):
    grouped = volume.astype(jnp.float32).reshape(volume.shape[:3] + (GROUPS, -1))
    entry_count = (
        volume.shape[0]
        * volume.shape[1]
        * lax.axis_size("row")
        * volume.shape[2]
        * grouped.shape[4]
    )
    group_total = lax.psum(jnp.sum(grouped, axis=(0, 1, 2, 4)), "row")
    group_avg = group_total / entry_count
    centred = grouped - group_avg[:, None]
    variance = lax.psum(jnp.sum(centred * centred, axis=(0, 1, 2, 4)), "row") / entry_count
    normal_part = centred * lax.rsqrt(variance + norm_eps)[:, None]
    return normal_part.reshape(volume.shape) * gain


def per_device(latent, w_in, gain_in, w_query, w_key, w_value, w_out, gain_up, w_up):
    frame_count, row_count, col_count, _ = latent.shape
    chan_width = w_query.shape[0]
    rimmed = extended(latent, (("row", 1),), 1)
    first_out = jnp.dot(
        tap_windows(pad_field(rimmed), frame_count, row_count, col_count),
        w_in.reshape(-1, chan_width),
        preferred_element_type=jnp.float32,
    )
    first_out = first_out.astype(jnp.bfloat16).reshape(
        frame_count, row_count, col_count, chan_width
    )
    normed = group_norm(first_out, gain_in).astype(jnp.bfloat16)
    flat_rows = normed.reshape(-1, chan_width)
    queries = jnp.dot(flat_rows, w_query, preferred_element_type=jnp.float32).astype(jnp.bfloat16)
    queries = queries.reshape(frame_count, row_count * col_count, chan_width)
    score_scale = 1.0 / math.sqrt(chan_width)
    key_table = jnp.dot(flat_rows, w_key, preferred_element_type=jnp.float32).astype(jnp.bfloat16)
    value_table = jnp.dot(flat_rows, w_value, preferred_element_type=jnp.float32).astype(
        jnp.bfloat16
    )
    key_table = key_table.reshape(frame_count, row_count, col_count, chan_width)
    value_table = value_table.reshape(frame_count, row_count, col_count, chan_width)
    row_peak = jnp.full((frame_count, row_count * col_count), -jnp.inf, jnp.float32)
    denom = jnp.zeros((frame_count, row_count * col_count), jnp.float32)
    weighted = jnp.zeros((frame_count, row_count * col_count, chan_width), jnp.float32)
    scores = (
        jnp.einsum(
            "fqd,fkd->fqk",
            queries,
            lax.all_gather(key_table, "row", axis=1, tiled=True).reshape(
                frame_count, -1, chan_width
            ),
            preferred_element_type=jnp.float32,
        )
        * score_scale
    )
    new_peak = jnp.max(scores, axis=-1)
    correction = jnp.exp(row_peak - new_peak)
    expo = jnp.exp(scores - new_peak[..., None])
    denom = denom * correction + jnp.sum(expo, axis=-1)
    weighted = weighted * correction[..., None] + jnp.einsum(
        "fqk,fkd->fqd",
        expo.astype(jnp.bfloat16),
        lax.all_gather(value_table, "row", axis=1, tiled=True).reshape(frame_count, -1, chan_width),
        preferred_element_type=jnp.float32,
    )
    row_peak, denom, weighted = (new_peak, denom, weighted)
    attended = (weighted / denom[..., None]).astype(jnp.bfloat16).reshape(-1, chan_width)
    added = first_out.astype(jnp.float32).reshape(-1, chan_width) + jnp.dot(
        attended, w_out, preferred_element_type=jnp.float32
    )
    added = added.astype(jnp.bfloat16).reshape(frame_count, row_count, col_count, chan_width)
    full_up = lax.all_gather(w_up, "row", axis=1, tiled=True)
    upsampled = jnp.repeat(jnp.repeat(added, 2, axis=1), 2, axis=2)
    up_rimmed = extended(upsampled, (("row", 1),), 1)
    padded_up = pad_field(up_rimmed)
    running = tap_products(padded_up, full_up, frame_count, 2 * row_count, 2 * col_count)
    convolved = running.astype(jnp.bfloat16).reshape(
        frame_count, 2 * row_count, 2 * col_count, chan_width
    )
    return jax.nn.silu(group_norm(convolved, gain_up)).astype(jnp.bfloat16)


LANES = 128
MIB = 1024 * 1024


def lane_iota(width):
    return lax.broadcasted_iota(jnp.int32, (1, width), 1)


def swap_blocks(arrays, width):
    arrays = list(arrays)
    block = lane_iota(LANES) // width
    step = 1
    while step < len(arrays):
        low = (block & step) == 0
        for t in range(len(arrays)):
            if t & step == 0:
                a, b = arrays[t], arrays[t | step]
                arrays[t] = jnp.where(low, a, pltpu.roll(b, step * width, 1))
                arrays[t | step] = jnp.where(low, pltpu.roll(a, LANES - step * width, 1), b)
        step *= 2
    return arrays


def group_sum(row, group):
    width = row.shape[1]
    lane = lane_iota(width)
    step = 1
    while step < group:
        low = (lane & step) == 0
        row = row + jnp.where(
            low, pltpu.roll(row, width - step, 1), pltpu.roll(row, step, 1)
        )
        step *= 2
    return row


def fold_rows(block):
    return jnp.sum(block.reshape(-1, 8, block.shape[1]), axis=0)


def all_rows(part):
    return jnp.broadcast_to(jnp.sum(part, axis=0, keepdims=True), part.shape)


def tap_tiles(taps, blocks):
    whole, rest = taps // blocks, taps % blocks
    tiles = [[(h, t * blocks + k) for k in range(blocks)] for h in range(2) for t in range(whole)]
    tail = []
    for h in range(2):
        tail += [(h, whole * blocks + k) for k in range(rest)]
        tail += [None] * (blocks // 2 - rest)
    return tiles + [tail]


def pack_kernel(w_any, out_any, w_ref, out_ref, sems, out_sems):
    taps, _, width = w_ref.shape
    groups, devices, depth, _ = out_ref.shape
    share = width // devices
    blocks = LANES // share
    first = pl.multiple_of(lax.axis_index("grp") * width, LANES)
    copies, outs = [], []
    for g in range(sems.shape[0]):
        at = slice(g * blocks, min((g + 1) * blocks, taps))
        copies.append(
            pltpu.make_async_copy(
                w_any.at[at, :, pl.ds(first, width)], w_ref.at[at], sems.at[g]
            )
        )
        copies[-1].start()
    tiles = tap_tiles(taps, blocks)
    loaded = 0
    for g in sorted(range(groups), key=lambda g: max(unit[1] for unit in tiles[g] if unit)):
        while loaded * blocks <= max(unit[1] for unit in tiles[g] if unit):
            copies[loaded].wait()
            loaded += 1
        for col in range(width // LANES):
            pieces = [
                jnp.zeros((depth, LANES), jnp.float32)
                if unit is None
                else w_ref[
                    unit[1],
                    unit[0] * depth : (unit[0] + 1) * depth,
                    col * LANES : (col + 1) * LANES,
                ].astype(jnp.float32)
                for unit in tiles[g]
            ]
            for d, piece in enumerate(swap_blocks(pieces, share)):
                out_ref[g, col * blocks + d] = piece.astype(out_ref.dtype)
        outs.append(
            pltpu.make_async_copy(
                out_ref.at[g], out_any.at[:, :, g * LANES : (g + 1) * LANES], out_sems.at[g]
            )
        )
        outs[-1].start()
    for copy in outs:
        copy.wait()


def mid_kernel(
    dims, z_ref, spread_ref, w_in_ref, gain_ref, wq_any, wk_any, wv_any, wo_any, out_ref,
    x32, wide, edge, h_ref, q_ref, k_ref, v_ref, wq_ref, wk_ref, wv_ref, wo_ref, sems,
):
    pairs = ((wq_any, wq_ref), (wk_any, wk_ref), (wv_any, wv_ref), (wo_any, wo_ref))
    loads = [pltpu.make_async_copy(a, b, sems.at[k]) for k, (a, b) in enumerate(pairs)]
    for load in loads:
        load.start()
    frames, rows, _, cols, zc, chan, chunk = dims
    per_frame = rows * cols
    total = frames * per_frame
    step = per_frame // 2
    per_tile = LANES // zc
    block = lane_iota(LANES) // zc
    first_row = lax.axis_index("row") % 2 * rows
    half = LANES // frames
    for g in range(rows // per_tile):
        tile = jnp.concatenate(
            [z_ref[first_row + g * per_tile + i] for i in range(per_tile)], 0
        ).astype(jnp.float32)
        turned = tile.T
        for f in range(frames):
            field = turned[f * half : f * half + cols]
            for i in range(per_tile):
                at = f * per_frame + (g * per_tile + i) * cols
                x32[at : at + cols, :] = jnp.where(block == i, field, 0.0).astype(x32.dtype)

    lane = lane_iota(edge.shape[2])
    col_tap = (lane // zc) % 3
    row_tap = (lane // zc) // 3
    blank = jnp.zeros((cols, edge.shape[2]), jnp.float32)
    col_index = lax.broadcasted_iota(jnp.int32, (cols, 1), 0)

    for f in range(frames):
        edge[f, 0:cols, :] = blank
        edge[f, (rows + 1) * cols : (rows + 2) * cols, :] = blank

        def columns(c, _):
            at = pl.multiple_of(f * per_frame + c * step, 16)
            v = jnp.dot(
                x32[pl.ds(at, step), :], spread_ref[...], preferred_element_type=jnp.float32
            )
            for k in range(step // cols):
                u = v[k * cols : (k + 1) * cols]
                before = jnp.where(col_index == 0, 0.0, pltpu.roll(u, 1, 0))
                after = jnp.where(col_index == cols - 1, 0.0, pltpu.roll(u, cols - 1, 0))
                u = jnp.where(col_tap == 0, before, jnp.where(col_tap == 2, after, u))
                edge[f, pl.ds(pl.multiple_of(c * step + (k + 1) * cols, 8), cols), :] = u
            return 0

        lax.fori_loop(0, per_frame // step, columns, 0)

        def lines(i, _):
            at = pl.multiple_of(i * cols, 8)
            above = edge[f, pl.ds(at, cols), :]
            here = edge[f, pl.ds(pl.multiple_of(at + cols, 8), cols), :]
            below = edge[f, pl.ds(pl.multiple_of(at + 2 * cols, 8), cols), :]
            v = jnp.where(row_tap == 0, above, jnp.where(row_tap == 2, below, here))
            wide[pl.ds(pl.multiple_of(f * per_frame + at, 16), cols), :] = v.astype(wide.dtype)
            return 0

        lax.fori_loop(0, rows, lines, 0, unroll=2)

    depth = wide.shape[1]

    def first(part):
        for f in range(frames):
            acc = None
            for dt in range(3):
                source = max(f + dt - 2, 0)
                at = source * per_frame
                term = jnp.dot(
                    wide[at : at + per_frame, :],
                    w_in_ref[dt * depth : (dt + 1) * depth, :],
                    preferred_element_type=jnp.float32,
                )
                acc = term if acc is None else acc + term
            acc = acc.astype(jnp.bfloat16)
            h_ref[slice(f * per_frame, (f + 1) * per_frame), :] = acc
            part = part + fold_rows(acc.astype(jnp.float32))
        return part

    zero = jnp.zeros((8, chan), jnp.float32)
    part = first(zero)
    group = chan // GROUPS
    count = total * group
    mean = group_sum(all_rows(part), group) / count
    mean_row = mean[0:1]

    def spreadness(c, part):
        v = h_ref[pl.ds(pl.multiple_of(c * chunk, 16), chunk), :].astype(jnp.float32) - mean_row
        return part + fold_rows(v * v)

    part = lax.fori_loop(0, total // chunk, spreadness, zero)
    variance = group_sum(all_rows(part), group) / count
    scale_row = lax.rsqrt(variance + norm_eps)[0:1]
    gain_row = gain_ref[...]

    for load in loads:
        load.wait()

    def project(c, _):
        at = pl.ds(pl.multiple_of(c * chunk, 16), chunk)
        v = h_ref[at, :].astype(jnp.float32) - mean_row
        normed = (v * scale_row * gain_row).astype(jnp.bfloat16)
        for w, o in ((wq_ref, q_ref), (wk_ref, k_ref), (wv_ref, v_ref)):
            o[at, :] = jnp.dot(normed, w[...], preferred_element_type=jnp.float32).astype(
                jnp.bfloat16
            )
        return 0

    lax.fori_loop(0, total // chunk, project, 0, unroll=total // chunk)
    score_scale = 1.0 / math.sqrt(chan)

    for f in range(frames):
        at = slice(f * per_frame, (f + 1) * per_frame)
        span = slice(f * per_frame, (f + 1) * per_frame)
        scores = lax.dot_general(
            q_ref[at, :],
            k_ref[span, :],
            (((1,), (1,)), ((), ())),
            preferred_element_type=jnp.float32,
        )
        peak = jnp.max(scores, axis=-1, keepdims=True)
        expo = jnp.exp2((scores - peak) * (score_scale * math.log2(math.e)))
        denom = jnp.sum(expo, axis=-1, keepdims=True)
        mixed = jnp.dot(
            expo.astype(jnp.bfloat16), v_ref[span, :], preferred_element_type=jnp.float32
        )
        mixed = (mixed * (1.0 / denom)).astype(jnp.bfloat16)
        shifted = jnp.dot(mixed, wo_ref[...], preferred_element_type=jnp.float32)
        out_ref[at, :] = (h_ref[at, :].astype(jnp.float32) + shifted).astype(jnp.bfloat16)


def fold_taps(w_ref, all_ref, new_ref, s_all, s_new, share):
    blocks = LANES // share
    width = s_all.shape[1]
    whole = 27 // blocks
    lane = lane_iota(width)
    inner, shift = (lane // share) % blocks, lane // LANES
    later, p, q = inner // 4 == 1, (inner // 2) % 2, inner % 2
    same = lax.broadcasted_iota(jnp.int32, (share, width), 0) == lane % share
    s_all[whole * LANES :, :] = jnp.zeros((2 * LANES, width), s_all.dtype)
    s_new[...] = jnp.zeros_like(s_new)
    for di in range(3):
        for dj in range(3):
            down = (di == 2) & (p == 1) | (di == 0) & (p == 0)
            along = (dj == 2) & (q == 1) | (dj == 0) & (q == 0)
            wanted = 2 * down.astype(jnp.int32) + along.astype(jnp.int32)
            fits_here = same & (shift == wanted)
            both, early, late = (
                jnp.where(v, 1.0, 0.0).astype(s_all.dtype)
                for v in (fits_here, fits_here & ~later, fits_here & later)
            )
            for dt in range(3):
                tap = 9 * dt + 3 * di + dj
                if tap < whole * blocks:
                    s_all[tap * share : (tap + 1) * share, :] = early if dt == 2 else both
                    if dt == 2:
                        at = (tap - (whole - 1) * blocks) * share
                        s_new[at : at + share, :] = late
                else:
                    for h in range(2):
                        at = h * (LANES + LANES // 2) + (tap - whole * blocks) * share
                        s_all[whole * LANES + at : whole * LANES + at + share, :] = early
                        s_new[LANES + at : LANES + at + share, :] = late
    tail = slice(2 * whole * LANES, (2 * whole + 1) * LANES)
    for h in range(2):
        main = slice(h * whole * LANES, (h + 1) * whole * LANES)
        last = slice(((h + 1) * whole - 1) * LANES, (h + 1) * whole * LANES)
        side = slice((whole + h) * LANES, (whole + h + 1) * LANES)
        new_side = slice((1 + h) * LANES, (2 + h) * LANES)
        for (lanes, s_ref, rows, side_rows), to_ref in (
            ((main, s_all, slice(0, whole * LANES), side), all_ref),
            ((last, s_new, slice(0, LANES), new_side), new_ref),
        ):
            v = jnp.dot(w_ref[:, lanes], s_ref[rows, :], preferred_element_type=jnp.float32)
            v += jnp.dot(w_ref[:, tail], s_ref[side_rows, :], preferred_element_type=jnp.float32)
            v = v.astype(to_ref.dtype)
            for k in range(v.shape[0] // share):
                at = (2 * k + h) * share
                to_ref[at : at + share, :] = v[k * share : (k + 1) * share]


def over_blocks(row, share):
    step = share
    while step < LANES:
        row = row + pltpu.roll(row, step, 1)
        step *= 2
    return row


def gain_kernel(share, gain_ref, out_ref):
    chan = gain_ref.shape[1]
    me = lax.axis_index("grp") * lax.axis_size("row") + lax.axis_index("row")
    gains = jnp.broadcast_to(gain_ref[...], (8, chan))
    gains = jnp.where(lane_iota(chan) // share == me, gains, 0.0)
    gains = sum(gains[:, k : k + LANES] for k in range(0, chan, LANES))
    out_ref[...] = over_blocks(gains, share)


def up_video(dims, ready, x_ref, all_ref, new_ref, gain_ref, t_ref, m0_ref, m2_ref, store):
    rows, cols, chan, share, _ = dims
    per_frame = rows * cols
    width = LANES

    ready(0)
    t_ref[...] = jnp.dot(
        x_ref[0:per_frame, :], all_ref[...], preferred_element_type=jnp.float32
    )
    ready(1)
    t_ref[...] += jnp.dot(
        x_ref[per_frame : 2 * per_frame, :], new_ref[...], preferred_element_type=jnp.float32
    )
    lane = lane_iota(width)
    right = (lane // share) % 2 == 1
    lower = (lane // (2 * share)) % 2 == 1
    col_index = lax.broadcasted_iota(jnp.int32, (cols, 1), 0)

    def beside(v):
        before = jnp.where(col_index == 0, 0.0, pltpu.roll(v, 1, 0))
        after = jnp.where(col_index == cols - 1, 0.0, pltpu.roll(v, cols - 1, 0))
        return jnp.where(right, after, before)

    blank = jnp.zeros((cols, width), jnp.float32)
    m2_ref[0:cols, :] = blank
    m2_ref[(rows + 1) * cols : (rows + 2) * cols, :] = blank

    def columns(i, _):
        at = pl.ds(pl.multiple_of(i * cols, 8), cols)
        m0_ref[at, :] = t_ref[at, 0:width] + beside(t_ref[at, width : 2 * width])
        m2_ref[pl.ds(pl.multiple_of((i + 1) * cols, 8), cols), :] = t_ref[
            at, 2 * width : 3 * width
        ] + beside(t_ref[at, 3 * width : 4 * width])
        return 0

    lax.fori_loop(0, rows, columns, 0, unroll=rows)

    def lines(i, part):
        at = pl.ds(pl.multiple_of(i * cols, 8), cols)
        above = m2_ref[at, :]
        below = m2_ref[pl.ds(pl.multiple_of((i + 2) * cols, 8), cols), :]
        v = m0_ref[at, :] + jnp.where(lower, below, above)
        v = v.astype(jnp.bfloat16).astype(jnp.float32)
        m0_ref[at, :] = v
        return part + fold_rows(v)

    part = lax.fori_loop(0, rows, lines, jnp.zeros((8, width), jnp.float32), unroll=rows)
    group = chan // GROUPS
    count = 2 * rows * cols * 4 * group

    def grouped(part):
        return group_sum(over_blocks(all_rows(part), share), group)

    mean_row = (grouped(part) / count)[0:1]

    def spreadness(i, part):
        v = m0_ref[pl.ds(pl.multiple_of(i * cols, 8), cols), :] - mean_row
        return part + fold_rows(v * v)

    part = lax.fori_loop(0, rows, spreadness, jnp.zeros((8, width), jnp.float32), unroll=rows)
    variance = grouped(part) / count
    scale_row = (lax.rsqrt(variance + norm_eps) * gain_ref[...])[0:1]

    def finish(d, _):
        at = pl.ds(pl.multiple_of(d * cols, 8), cols)
        v = (m0_ref[at, :] - mean_row) * scale_row
        store(d, v / (1.0 + jnp.exp(-v)))
        return 0

    lax.fori_loop(0, rows, finish, 0, unroll=rows)


def near_kernel(
    dims, w_ref, x_ref, gain_ref, out_ref, all_ref, new_ref, t_ref, m0_ref, m2_ref, s_all, s_new
):
    fold_taps(w_ref, all_ref, new_ref, s_all, s_new, dims[3])

    def store(d, v):
        out_ref[d] = v.astype(out_ref.dtype)

    def ready(f):
        pass

    up_video(dims, ready, x_ref, all_ref, new_ref, gain_ref, t_ref, m0_ref, m2_ref, store)


def far_kernel(
    dims, near_ref, x_any, all_ref, new_ref, gain_ref, out_ref, t_ref, m0_ref, m2_ref, x_ref, sems
):
    rows, cols = dims[:2]
    loads = []
    for f in range(2):
        at = slice(f * rows * cols, (f + 1) * rows * cols)
        loads.append(pltpu.make_async_copy(x_any.at[at], x_ref.at[at], sems.at[f]))
        loads[-1].start()
    video = lax.axis_index("row") % 2

    def keep(d, _):
        out_ref[video * rows + d] = near_ref[d]
        return 0

    lax.fori_loop(0, rows, keep, 0, unroll=4)

    def store(d, v):
        out_ref[(1 - video) * rows + d] = v.astype(out_ref.dtype)

    def ready(f):
        loads[f].wait()

    up_video(dims, ready, x_ref, all_ref, new_ref, gain_ref, t_ref, m0_ref, m2_ref, store)


def place_kernel(share, x_ref, out_any, line, out_ref, sems):
    devices = x_ref.shape[0]
    blocks = LANES // share
    cols = x_ref.shape[1]
    outs = []
    for a in range(devices // blocks):
        pieces = swap_blocks(
            [x_ref[a * blocks + k].astype(jnp.float32) for k in range(blocks)], share
        )
        for half in range(blocks // 2):
            slot = a * (blocks // 2) + half
            for q in range(2):
                line[slot, pl.ds(q, cols, stride=2), :] = pieces[2 * half + q]
            out_ref[a, half // 2, half % 2] = line[slot].astype(out_ref.dtype)
        outs.append(
            pltpu.make_async_copy(
                out_ref.at[a], out_any.at[:, :, :, a * LANES : (a + 1) * LANES], sems.at[a]
            )
        )
        outs[-1].start()
    for copy in outs:
        copy.wait()


def fits(mesh, shapes):
    latent, w_query = shapes
    count = mesh.shape["row"]
    frames, own, cols, zc = latent
    chan = w_query[0]
    rows = own * count
    share = chan // (2 * count)
    return (
        mesh.shape["grp"] == 2
        and frames == 2
        and own == 1
        and count >= 8
        and count & (count - 1) == 0
        and share == 16
        and chan == 2 * count * share
        and chan == GROUPS * share
        and zc == 16
        and cols % 16 == 0
        and cols <= LANES // frames
        and (rows * cols) % 256 == 0
        and rows * cols <= 1024
    )


def call(kernel, out_shape, scratch, limit, flops, moved, spaces, out_space=pltpu.VMEM):
    return pl.pallas_call(
        kernel,
        out_shape=out_shape,
        in_specs=[pl.BlockSpec(memory_space=space) for space in spaces],
        out_specs=jax.tree.map(lambda space: pl.BlockSpec(memory_space=space), out_space),
        scratch_shapes=scratch,
        compiler_params=pltpu.CompilerParams(vmem_limit_bytes=limit * MIB),
        cost_estimate=pl.CostEstimate(flops=flops, bytes_accessed=moved, transcendentals=0),
    )


def whole_video(latent, w_in, gain_in, w_query, w_key, w_value, w_out, gain_up, w_up):
    frames, own, cols, zc = latent.shape
    chan = w_query.shape[0]
    count = lax.axis_size("row")
    rows = own * count
    positions = frames * rows * cols
    share = chan // (2 * count)
    blocks = LANES // share
    tiles = len(tap_tiles(27, blocks))
    f32, bf16 = jnp.float32, jnp.bfloat16
    shape = jax.ShapeDtypeStruct
    chunk = 256

    half = LANES // frames
    cells = jnp.swapaxes(latent.reshape(frames, cols, zc), 1, 2)
    cells = jnp.pad(cells, ((0, 0), (0, 0), (0, half - cols)))
    cells = jnp.concatenate([cells[f] for f in range(frames)], 1)
    cells = jnp.broadcast_to(cells, (2 * count, zc, LANES))
    cells = lax.all_to_all(cells, ("grp", "row"), 0, 0, tiled=True)

    pack = call(
        pack_kernel,
        shape((count, share, tiles * LANES), bf16),
        [
            pltpu.VMEM((27, 2 * share, count * share), bf16),
            pltpu.VMEM((tiles, count, share, LANES), bf16),
            pltpu.SemaphoreType.DMA((-(-27 // blocks),)),
            pltpu.SemaphoreType.DMA((tiles,)),
        ],
        8,
        10**6,
        2 * 10**6,
        (pltpu.HBM,),
        pltpu.HBM,
    )
    packed = pack(pltpu.with_memory_space_constraint(w_up, pltpu.HBM))
    weights = lax.all_to_all(packed, "row", 0, 0, tiled=True)
    weights = weights.reshape(chan // 2, tiles * LANES)

    depth = 9 * zc
    spread = np.zeros((LANES, depth), np.float32)
    for k in range(LANES):
        for t in range(9):
            spread[k, t * zc + k % zc] = 1.0
    dims = (frames, rows, own, cols, zc, chan, chunk)
    middle = call(
        functools.partial(mid_kernel, dims),
        shape((positions, chan), bf16),
        [
            pltpu.VMEM((positions, LANES), bf16),
            pltpu.VMEM((positions, depth), bf16),
            pltpu.VMEM((frames, (rows + 2) * cols, depth), f32),
        ]
        + [pltpu.VMEM((positions, chan), bf16)] * 4
        + [pltpu.VMEM((chan, chan), bf16)] * 4
        + [pltpu.SemaphoreType.DMA((4,))],
        28,
        7 * 10**9,
        6 * 10**6,
        (pltpu.VMEM,) * 4 + (pltpu.HBM,) * 4,
    )
    added = middle(
        cells,
        jnp.asarray(spread, bf16),
        w_in.reshape(3 * depth, chan),
        gain_in.reshape(1, chan),
        *(
            pltpu.with_memory_space_constraint(w, pltpu.HBM)
            for w in (w_query, w_key, w_value, w_out)
        ),
    )

    dims = (rows, cols, chan, share, chunk)
    width = 4 * LANES
    gains = call(
        functools.partial(gain_kernel, share), shape((8, LANES), f32), [], 1, 10**4, 10**4,
        (pltpu.VMEM,),
    )
    gain = gains(gain_up.reshape(1, chan))
    fields = [
        pltpu.VMEM((rows * cols, width), f32),
        pltpu.VMEM((rows * cols, LANES), f32),
        pltpu.VMEM(((rows + 2) * cols, LANES), f32),
    ]
    fold = shape((chan, width), bf16)
    first = call(
        functools.partial(near_kernel, dims),
        (shape((count, cols, LANES), bf16), fold, fold),
        fields + [pltpu.VMEM((5 * LANES, width), bf16), pltpu.VMEM((3 * LANES, width), bf16)],
        16,
        2 * 10**9,
        3 * 10**6,
        (pltpu.VMEM,) * 3,
        (pltpu.VMEM,) * 3,
    )
    near_out, fold_all, fold_new = first(weights, added, gain)
    other = lax.ppermute(added, "row", [(k, k ^ 1) for k in range(count)])
    decoded = call(
        functools.partial(far_kernel, dims),
        shape((2 * count, cols, LANES), bf16),
        fields + [pltpu.VMEM(added.shape, bf16), pltpu.SemaphoreType.DMA((2,))],
        16,
        2 * 10**9,
        3 * 10**6,
        (pltpu.VMEM, pltpu.HBM) + (pltpu.VMEM,) * 3,
    )(near_out, pltpu.with_memory_space_constraint(other, pltpu.HBM), fold_all, fold_new, gain)
    swapped = lax.all_to_all(decoded, ("grp", "row"), 0, 0, tiled=True)
    return call(
        functools.partial(place_kernel, share),
        shape((frames, 2 * own, 2 * cols, chan), bf16),
        [
            pltpu.VMEM((2 * count // 2, 2 * cols, LANES), f32),
            pltpu.VMEM((chan // LANES, frames, 2 * own, 2 * cols, LANES), bf16),
            pltpu.SemaphoreType.DMA((chan // LANES,)),
        ],
        8,
        10**6,
        10**6,
        (pltpu.VMEM,),
        pltpu.HBM,
    )(swapped)


def solution(mesh):
    def body(*args):
        whole = fits(mesh, (args[0].shape, args[3].shape))
        return (whole_video if whole else per_device)(*args)

    in_specs = (
        P("grp", "row", None, None),
        P(),
        P(),
        P(),
        P(),
        P(),
        P(),
        P(),
        P(None, "row", None),
    )
    out_specs = P("grp", "row", None, None)
    return jax.shard_map(
        body, mesh=mesh, in_specs=in_specs, out_specs=out_specs, check_vma=False
    )
```
